128 devices in a mesh: row: 8 (over z, core), col: 16 (over x, y).
Axes of the slice: x: 4, y: 4, z: 4, core: 2. Of those that a mesh axis runs over, the one named last changes fastest.
Arguments:
- a_blocks: float32 [1024, 8, 256, 256], P(('row', 'col')), may hold values from -0.09375 to 0.09375
- a_live: int32 [1024, 8], P(('row', 'col')), may hold values from 0 to 1, as said below
- p_blocks: float32 [1024, 256, 2, 128], P(('row', 'col')), may hold values from -0.1875 to 0.1875
- p_cols: int32 [1024, 2], P(('row', 'col')), may hold values from 0 to 127, as said below
- ghost_list: int32 [1024, 7], P(('row', 'col')), may hold values from 0 to 7, as said below
- policy: int32 [1024], P(('row', 'col')), may hold values from 0 to 15
- rates: float32 [16, 256], replicated, may hold values from 0.1 to 1
- rhs: float32 [16384, 256], P(('row', 'col')), may hold values from -6 to 6
- guess: float32 [16384, 256], P(('row', 'col')), may hold values from -6 to 6
Outputs:
- coarse: float32 [16384, 8, 16, 128], P('row', None, 'col')
- smoothed: float32 [16384, 256], P(('row', 'col'))
The draws below stay inside these ranges and needn't reach their ends.
Inputs may be any that keep to these rules, and one draw needn't show every extreme that they name: a_live[i, 0] is 1 for every i. On each device and for each k, the entries ghost_list[d * 8 + s, k] over s = 0 .. 7 are a permutation of 0 .. 7. p_cols[j, m] modulo the number of col devices equals (col index of the device holding block row j + m * 8) modulo that number. The quotient by that number names a mesh row: among the 16 entries of one device at most 2 name the same mesh row, and the device's own mesh row is named exactly 2 times, by at least one entry of each m.
All inputs are finite; a program needn't handle non-finite values.
Results may differ from the reference program's by a relative error of at most 0.0003.
Values sent between devices are 32-bit elements; how exact they have to be, the bound alone decides.
No kernel may reach another device: no remote copies, remote signals or barrier semaphores. Data moves between devices by JAX's collectives and lax.ppermute only.
A program may use at most 192 MiB of HBM per device.

```python
import math
import jax
import jax.numpy as jnp
from jax import lax

BS = 256
CB = 128
KA = 8
KP = 2
NPOL = 16
NCOL = 256
NB = 8
NFB = 1024
NC = 16384
RCAP = 2
N_ROW = 8
N_COL = 16
DEVICES = 128


def pattern(key):
    base = jax.random.fold_in(key, 1301)
    key_perm, key_pad, key_pick, key_score, key_rest = jax.random.split(base, 5)
    device = jnp.arange(DEVICES, dtype=jnp.int32)
    row_of = device // N_COL
    col_of = device % N_COL
    within = jnp.arange(NB, dtype=jnp.int32)
    perm_keys = jax.random.randint(key_perm, (DEVICES, KA - 1, NB), 0, 1 << 20) * NB + within
    orders = jnp.argsort(perm_keys, axis=-1).astype(jnp.int32)
    ghost = orders.transpose(0, 2, 1).reshape(NFB, KA - 1)
    padding = jax.random.randint(key_pad, (NFB, KA - 1), 0, 8)
    live = jnp.concatenate([jnp.ones((NFB, 1), jnp.int32), (padding != 0).astype(jnp.int32)], axis=1)
    pair_count = NB * KP
    pair = jnp.arange(pair_count, dtype=jnp.int32)
    pair_m = pair % KP
    pair_t = pair // KP
    first_t = jax.random.randint(key_pick, (DEVICES, KP), 0, NB)
    chosen = pair_t[None, :] == first_t[:, pair_m]
    score = jax.random.randint(key_score, (DEVICES, pair_count), 0, 1 << 20) * pair_count + pair
    score = jnp.where(chosen, -1 - pair[None, :], score)
    ranks = jnp.argsort(jnp.argsort(score, axis=1), axis=1).astype(jnp.int32)
    forced = ranks < RCAP
    pool_size = (N_ROW - 1) * RCAP
    places = jnp.arange(pool_size, dtype=jnp.int32)
    pool_vals = (row_of[:, None] + 1 + places[None, :] // RCAP) % N_ROW
    pool_keys = jax.random.randint(key_rest, (DEVICES, pool_size), 0, 1 << 20) * pool_size + places
    shuffled = jnp.take_along_axis(pool_vals, jnp.argsort(pool_keys, axis=1), axis=1)
    others = jnp.take_along_axis(shuffled, jnp.clip(ranks - RCAP, 0, pool_size - 1), axis=1)
    groups = jnp.where(forced, row_of[:, None], others)
    coarse_cols = N_COL * groups + (col_of[:, None] + pair_m[None, :] * KA) % N_COL
    return (live, coarse_cols.reshape(NFB, KP).astype(jnp.int32), ghost)


def draw_a_live(key, part):
    return pattern(key)[0]


def draw_p_cols(key, part):
    return pattern(key)[1]


def draw_ghost_list(key, part):
    return pattern(key)[2]


def place_ends(drawn, key, smallest, high):
    dims = drawn.shape
    place = [jax.random.randint(jax.random.fold_in(key, axis), (), 0, dims[axis]) for axis in range(len(dims))]
    drawn = drawn.at[tuple(place)].set(smallest)
    longest = dims.index(max(dims))
    place[longest] = (place[longest] + 1) % dims[longest]
    return drawn.at[tuple(place)].set(high)


def levels(key, shape, cuts, least, top_value):
    factor_of = 1.0
    for axis_at, blocks in cuts:
        heights = jax.random.uniform(jax.random.fold_in(jax.random.fold_in(key, 6), axis_at), (blocks,), jnp.float32, least / len(cuts), top_value / len(cuts))
        factor_of = factor_of * jnp.repeat(jnp.exp(heights), shape[axis_at] // blocks).reshape((-1,) + (1,) * (len(shape) - 1 - axis_at))
    return factor_of


def noise(own_key, extent, deviation, most, cuts=(), held_as=jnp.bfloat16):
    loudness = levels(own_key, extent, cuts, -0.22, 0.18) if cuts else 1.0
    drawn = jax.random.normal(own_key, extent, jnp.float32) * deviation * loudness
    return jnp.minimum(jnp.maximum(drawn, -most), most).astype(held_as)


def setup_inputs(seed: int = 0) -> dict:
    key_of = jax.random.split(jax.random.key(seed), 10)
    a_blocks = noise(key_of[0], (NFB, KA, BS, BS), 0.015625, 0.09375, ((0, 128),), jnp.float32)
    a_live = draw_a_live(jax.random.fold_in(key_of[9], 71), 0)
    p_blocks = noise(key_of[2], (NFB, BS, KP, CB), (4 * BS) ** -0.5, 0.1875, ((0, 128),), jnp.float32)
    p_cols = draw_p_cols(jax.random.fold_in(key_of[9], 71), 0)
    ghost_list = draw_ghost_list(jax.random.fold_in(key_of[9], 71), 0)
    policy = place_ends(jax.random.randint(key_of[5], (NFB,), 0, NPOL), jax.random.fold_in(key_of[5], 1), 0, NPOL - 1).astype(jnp.int32)
    rates = jnp.clip(jnp.exp(jax.random.uniform(key_of[6], (NPOL, BS), jnp.float32, math.log(0.1), math.log(1.0))), 0.1, 1.0)
    rhs = noise(key_of[7], (NC, NCOL), 1.0, 6.0, ((0, 128),), jnp.float32)
    guess = noise(key_of[8], (NC, NCOL), 1.0, 6.0, ((0, 128),), jnp.float32)
    return {"a_blocks": a_blocks, "a_live": a_live, "p_blocks": p_blocks, "p_cols": p_cols, "ghost_list": ghost_list, "policy": policy, "rates": rates, "rhs": rhs, "guess": guess}


damping = 0.7


def reference(a_blocks, a_live, p_blocks, p_cols, ghost_list, policy, rates, rhs, guess):
    highest = lax.Precision.HIGHEST
    prolong = p_blocks.reshape(NFB, BS, KP * CB)
    later = jnp.arange(1, KA, dtype=jnp.int32)

    def one_row(coarse, index):
        device = index // NB
        within = index % NB
        source = (device // N_COL) * N_COL + (device % N_COL - later) % N_COL
        picks = source * NB + ghost_list[source * NB + within, later - 1]
        block_cols = jnp.concatenate([index[None], picks]).astype(jnp.int32)
        ghost = prolong[block_cols]
        ghost_cols = p_cols[block_cols]
        blocks = a_blocks[index] * a_live[index][:, None, None].astype(a_blocks.dtype)
        blocks = blocks.at[0].add(jnp.diag(rates[policy[index]]))
        product = jnp.einsum('kab,kbn->kan', blocks, ghost, precision=highest)
        partial_value = jnp.einsum('am,kan->kmn', prolong[index], product, precision=highest)
        partial_value = partial_value.reshape(KA, KP, CB, KP, CB).transpose(0, 1, 3, 2, 4)
        row_sel = jnp.broadcast_to(p_cols[index][None, :, None], (KA, KP, KP))
        col_sel = jnp.broadcast_to(ghost_cols[:, None, :], (KA, KP, KP))
        return coarse.at[row_sel, col_sel].add(partial_value), None

    start_blocks = jnp.zeros((DEVICES, DEVICES, CB, CB), jnp.float32)
    coarse, _ = lax.scan(one_row, start_blocks, jnp.arange(NFB, dtype=jnp.int32))
    matrix = coarse.transpose(0, 2, 1, 3).reshape(NC, NC)
    floor_diag = jnp.maximum(jnp.abs(jnp.diagonal(matrix)), 1.0)
    current = guess
    for sweep in range(2):
        applied = jnp.dot(matrix, current, precision=highest)
        current = current + damping * (rhs - applied) / floor_diag[:, None]
    return matrix.reshape(NC, N_ROW, N_COL, CB), current
```

```python
import functools

import jax
import jax.numpy as jnp
from jax import lax
from jax.experimental import pallas as pl
from jax.experimental.pallas import tpu as pltpu
from jax.sharding import PartitionSpec as P

BS = 256
CB = 128
KA = 8
KP = 2
N_ROW = 8
N_COL = 16
DEV = N_ROW * N_COL
NB = 8
NCOL = 256
damping = 0.7
f32 = jnp.float32
bf16 = jnp.bfloat16
ALL = ("row", "col")


def split(value):
    high = value.astype(bf16)
    return high, (value - high.astype(f32)).astype(bf16)


def dot3(lhs, rhs):
    dot = functools.partial(jnp.dot, preferred_element_type=f32)
    return dot(lhs[0], rhs[0]) + (dot(lhs[0], rhs[1]) + dot(lhs[1], rhs[0]))


def transpose_kernel(p_ref, high_ref, low_ref):
    for m in range(KP):
        high, low = split(p_ref[0, pl.ds(m, BS, KP), :].T)
        high_ref[0, m] = high
        low_ref[0, m] = low


def transposed(own_p):
    shape = jax.ShapeDtypeStruct((NB, KP, CB, BS), bf16)
    spec = pl.BlockSpec((1, KP, CB, BS), lambda s: (s, 0, 0, 0))
    return pl.pallas_call(
        transpose_kernel,
        grid=(NB,),
        in_specs=[pl.BlockSpec((1, KP * BS, CB), lambda s: (s, 0, 0))],
        out_specs=[spec, spec],
        out_shape=[shape, shape],
    )(own_p)


ROW_AT, SLOT_AT, POLICY_AT = 0, 16, 32
COL_AT, HALF_AT, PICK_AT, LIVE_AT = 40, 48, 56, 120


def product_kernel(first, with_prior, table, a_ref, p_ref, high_ref, low_ref, rate_ref, *rest):
    out_ref, q_high, q_low = rest[-3:]
    k = first + pl.program_id(0)
    s = pl.program_id(1)
    m = pl.program_id(2)

    @pl.when(m == 0)
    def _():
        block = a_ref[0, 0] * table[LIVE_AT + k * NB + s].astype(f32)
        if first == 0:
            across = lax.broadcasted_iota(jnp.int32, (BS, BS), 0)
            along = lax.broadcasted_iota(jnp.int32, (BS, BS), 1)
            rate = jnp.where((across == along) & (k == 0), rate_ref[0], 0.0)
            block = block + rate
        ghost = jnp.concatenate(
            [p_ref[0, pl.ds(0, BS, KP), :], p_ref[0, pl.ds(1, BS, KP), :]], axis=1
        )
        high, low = split(dot3(split(block), split(ghost)))
        q_high[...] = high
        q_low[...] = low

    result = dot3((high_ref[0, 0], low_ref[0, 0]), (q_high[...], q_low[...]))
    flip = table[HALF_AT + k] == 1
    left, right = result[:, :CB], result[:, CB:]
    out_ref[0, 0, 0, 0] = jnp.where(flip, right, left)
    out_ref[0, 1, 0, 0] = jnp.where(flip, left, right)


def products(first, count, table, a_blocks, source, high, low, rates, prior):
    in_specs = [
        pl.BlockSpec((1, 1, BS, BS), lambda k, s, m, t: (s, first + k, 0, 0)),
        pl.BlockSpec((1, KP * BS, CB), lambda k, s, m, t: (t[PICK_AT + (first + k) * NB + s], 0, 0)),
        pl.BlockSpec((1, 1, CB, BS), lambda k, s, m, t: (s, m, 0, 0)),
        pl.BlockSpec((1, 1, CB, BS), lambda k, s, m, t: (s, m, 0, 0)),
        pl.BlockSpec((1, 1, BS), lambda k, s, m, t: (t[POLICY_AT + s], 0, 0)),
    ]
    args = [a_blocks, source, high, low, rates]
    alias = {}
    if prior is not None:
        in_specs.append(pl.BlockSpec(memory_space=pl.ANY))
        args.append(prior)
        alias = {6: 0}
    return pl.pallas_call(
        functools.partial(product_kernel, first, prior is not None),
        grid_spec=pltpu.PrefetchScalarGridSpec(
            num_scalar_prefetch=1,
            grid=(count, NB, KP),
            in_specs=in_specs,
            out_specs=pl.BlockSpec(
                (1, 2, 1, 1, CB, CB),
                lambda k, s, m, t: (
                    t[ROW_AT + s * KP + m],
                    0,
                    t[COL_AT + first + k],
                    t[SLOT_AT + s * KP + m],
                    0,
                    0,
                ),
            ),
            scratch_shapes=[pltpu.VMEM((BS, BS), bf16), pltpu.VMEM((BS, BS), bf16)],
        ),
        out_shape=jax.ShapeDtypeStruct((N_ROW, 2, N_COL // 2, 2, CB, CB), f32),
        input_output_aliases=alias,
        cost_estimate=pl.CostEstimate(
            flops=count * NB * 2 * 3 * 2 * BS**3,
            bytes_accessed=count * NB * 4 * 3 * BS * BS,
            transcendentals=0,
        ),
    )(table, *args)


STEPS = 16
PER_STEP = 2 * DEV // STEPS


def gather_kernel(table, got_ref, x_ref, coarse_ref, part_ref, floor_ref, total):
    step = pl.program_id(0)

    @pl.when(step == 0)
    def _():
        total[...] = jnp.zeros_like(total)

    for b in range(PER_STEP):
        place = table[step * PER_STEP + b]
        total[place] += got_ref[b]

    @pl.when(step == STEPS - 1)
    def _():
        right = split(x_ref[...])

        @pl.loop(0, N_COL)
        def _(u):
            for q in range(N_ROW):
                coarse_ref[pl.ds(u * (CB * N_ROW) + q, CB, N_ROW), :] = total[u * N_ROW + q]
            row = jnp.concatenate([total[u * N_ROW + q] for q in range(N_ROW)], axis=1)
            part_ref[pl.ds(pl.multiple_of(u * CB, CB), CB), :] = dot3(split(row), right)

        across = lax.broadcasted_iota(jnp.int32, (CB, CB), 0)
        along = lax.broadcasted_iota(jnp.int32, (CB, CB), 1)
        own = jnp.where(across == along, total[table[2 * DEV]], 0.0)
        diag = jnp.maximum(jnp.abs(jnp.sum(own, axis=1, keepdims=True)), 1.0)
        floor_ref[...] = jnp.broadcast_to(diag, (CB, NCOL))


def gather(table, got, x):
    whole = lambda shape: pl.BlockSpec(shape, lambda i, t: (0,) * len(shape))
    return pl.pallas_call(
        gather_kernel,
        grid_spec=pltpu.PrefetchScalarGridSpec(
            num_scalar_prefetch=1,
            grid=(STEPS,),
            in_specs=[
                pl.BlockSpec((PER_STEP, CB, CB), lambda i, t: (i, 0, 0)),
                whole((N_ROW * CB, NCOL)),
            ],
            out_specs=[
                whole((N_COL * CB * N_ROW, CB)),
                whole((N_COL * CB, NCOL)),
                whole((CB, NCOL)),
            ],
            scratch_shapes=[pltpu.VMEM((DEV, CB, CB), f32)],
        ),
        out_shape=[
            jax.ShapeDtypeStruct((N_COL * CB * N_ROW, CB), f32),
            jax.ShapeDtypeStruct((N_COL * CB, NCOL), f32),
            jax.ShapeDtypeStruct((CB, NCOL), f32),
        ],
    )(table, got, x)


def apply_kernel(c_ref, x_ref, out_ref, x_high, x_low):
    @pl.when(pl.program_id(0) == 0)
    def _():
        high, low = split(x_ref[...])
        x_high[...] = high
        x_low[...] = low

    row = jnp.concatenate([c_ref[pl.ds(q, CB, N_ROW), :] for q in range(N_ROW)], axis=1)
    out_ref[...] = dot3(split(row), (x_high[...], x_low[...]))


def apply(coarse, x):
    return pl.pallas_call(
        apply_kernel,
        grid=(N_COL,),
        in_specs=[
            pl.BlockSpec((CB * N_ROW, CB), lambda u: (u, 0)),
            pl.BlockSpec((N_ROW * CB, NCOL), lambda u: (0, 0)),
        ],
        out_specs=pl.BlockSpec((CB, NCOL), lambda u: (u, 0)),
        out_shape=jax.ShapeDtypeStruct((N_COL * CB, NCOL), f32),
        scratch_shapes=[pltpu.VMEM((N_ROW * CB, NCOL), bf16)] * 2,
    )(coarse, x)


def to_all(value, axes, count):
    copies = jnp.broadcast_to(value[None], (count,) + value.shape)
    return lax.all_to_all(copies, axes, split_axis=0, concat_axis=0, tiled=True)


def own_table(p_cols, a_live, policy, metas, row, col):
    entry_row = (p_cols // N_COL).reshape(-1)
    order = jnp.arange(NB * KP, dtype=jnp.int32)
    slot = jnp.sum(
        (entry_row[None, :] == entry_row[:, None]) & (order[None, :] < order[:, None]),
        axis=1,
        dtype=jnp.int32,
    )
    k = jnp.arange(KA, dtype=jnp.int32)
    target = (col - k) % N_COL
    return entry_row, slot, target


def places(metas, row, col):
    delta = jnp.arange(N_COL, dtype=jnp.int32)
    p_cols = metas[:, :, :, :KP]
    entries = p_cols.reshape(N_ROW, N_COL, NB * KP)
    match = (entries // N_COL == row).astype(jnp.int32)
    earlier = jnp.cumsum(match, axis=2) - match
    order = jnp.arange(NB * KP, dtype=jnp.int32)
    sources = [
        lax.dynamic_index_in_dim(metas, (col + h * KA) % N_COL, 1, False) for h in range(2)
    ]
    result = []
    for t in range(2):
        chosen = match * (earlier == t)
        entry = jnp.sum(chosen * order, axis=2)
        u = jnp.sum(chosen * (entries % N_COL), axis=2)
        block = entry // KP
        far = (delta - col) % N_COL
        k, half = far % KA, far // KA
        quotient = jnp.zeros_like(u)
        for h in range(2):
            cells = sources[h]
            identity = jnp.broadcast_to(jnp.arange(NB, dtype=jnp.int32)[None, :, None], (N_ROW, NB, 1))
            picks = jnp.concatenate([identity, cells[:, :, KP:]], axis=2)
            hit = (block[:, :, None, None] == jnp.arange(NB)[None, None, :, None]) & (
                k[None, :, None, None] == jnp.arange(KA)[None, None, None, :]
            )
            pick = jnp.sum(jnp.where(hit, picks[:, None], 0), axis=(2, 3))
            value = jnp.sum(
                jnp.where(pick[:, :, None] == jnp.arange(NB), cells[:, None, :, h] // N_COL, 0), axis=2
            )
            quotient = jnp.where(half[None, :] == h, value, quotient)
        result.append(u * N_ROW + quotient)
    return jnp.stack(result, axis=2).reshape(-1)


def on_device(a_blocks, a_live, p_blocks, p_cols, ghost_list, policy, rates, rhs, guess):
    row = lax.axis_index("row")
    col = lax.axis_index("col")
    own_p = p_blocks.reshape(NB, BS * KP, CB)
    meta = jnp.concatenate([p_cols, ghost_list], axis=1)
    metas = to_all(meta.reshape(-1), ALL, DEV).reshape(N_ROW, N_COL, NB, KP + KA - 1)
    all_p = lax.all_gather(own_p, "col", axis=0, tiled=True)
    x = to_all(guess, "row", N_ROW).reshape(N_ROW * CB, NCOL)
    high, low = transposed(own_p)

    entry_row, slot, target = own_table(p_cols, a_live, policy, metas, row, col)
    mine = lax.dynamic_index_in_dim(metas, row, 0, False)
    picks = [jnp.arange(NB, dtype=jnp.int32) + col * NB]
    for k in range(1, KA):
        source = (col - k) % N_COL
        picks.append(lax.dynamic_index_in_dim(mine, source, 0, False)[:, KP + k - 1] + source * NB)
    table = jnp.concatenate(
        [entry_row, slot, policy, target % KA, target // KA, jnp.concatenate(picks), a_live.T.reshape(-1)]
    )
    sent = products(0, KA, table, a_blocks, all_p, high, low, rates.reshape(16, 1, BS), None)
    got = lax.all_to_all(
        sent.reshape(DEV, 2, CB, CB), ALL, split_axis=0, concat_axis=0, tiled=True
    ).reshape(2 * DEV, CB, CB)
    where = jnp.concatenate([places(metas, row, col), (col * N_ROW + row).reshape(1)])
    coarse, part, floor_diag = gather(where, got, x)
    current = guess
    for sweep in range(2):
        if sweep:
            part = apply(coarse, to_all(current, "row", N_ROW).reshape(N_ROW * CB, NCOL))
        pieces = lax.all_to_all(
            part.reshape(N_COL, CB, NCOL), "col", split_axis=0, concat_axis=0, tiled=True
        )
        applied = jnp.sum(pieces, axis=0)
        current = current + damping * (rhs - applied) / floor_diag
    return coarse.reshape(N_COL * CB, N_ROW, 1, CB), current


def solution(mesh):
    return jax.shard_map(
        on_device,
        mesh=mesh,
        in_specs=(
            P(ALL, None, None, None),
            P(ALL, None),
            P(ALL, None, None, None),
            P(ALL, None),
            P(ALL, None),
            P(ALL),
            P(),
            P(ALL, None),
            P(ALL, None),
        ),
        out_specs=(P("row", None, "col", None), P(ALL, None)),
        check_vma=False,
    )
```

```python
import functools

import jax
import jax.numpy as jnp
from jax import lax
from jax.experimental import pallas as pl
from jax.experimental.pallas import tpu as pltpu
from jax.sharding import Mesh, PartitionSpec as P

BS = 256
CB = 128
KA = 8
KP = 2
N_ROW = 8
N_COL = 16
DEV = N_ROW * N_COL
NB = 8
NCOL = 256
damping = 0.7
f32 = jnp.float32
bf16 = jnp.bfloat16
ROW = ("z", "core")
COL = ("x", "y")
ALL = ROW + COL
PLANE = ROW + ("x",)
N_X = N_Y = 4
GROUP = 4
PAIR = 2


def split(value):
    high = value.astype(bf16)
    return high, (value - high.astype(f32)).astype(bf16)


def dot3(lhs, rhs):
    dot = functools.partial(jnp.dot, preferred_element_type=f32)
    return dot(lhs[0], rhs[0]) + (dot(lhs[0], rhs[1]) + dot(lhs[1], rhs[0]))


def transpose_kernel(p_ref, high_ref, low_ref):
    for m in range(KP):
        high, low = split(p_ref[0, pl.ds(m, BS, KP), :].T)
        high_ref[0, m] = high
        low_ref[0, m] = low


def transposed(own_p):
    shape = jax.ShapeDtypeStruct((NB, KP, CB, BS), bf16)
    spec = pl.BlockSpec((1, KP, CB, BS), lambda s: (s, 0, 0, 0))
    return pl.pallas_call(
        transpose_kernel,
        grid=(NB,),
        in_specs=[pl.BlockSpec((1, KP * BS, CB), lambda s: (s, 0, 0))],
        out_specs=[spec, spec],
        out_shape=[shape, shape],
    )(own_p)


def left_kernel(group, table, a_ref, high_ref, low_ref, rate_ref, out_ref):
    s = pl.program_id(0)
    parts = []
    for k2 in range(PAIR):
        block = a_ref[0, k2, 0] * table[s * KA + group + GROUP * k2].astype(f32)
        if group == 0 and k2 == 0:
            across = lax.broadcasted_iota(jnp.int32, (BS, BS), 0)
            along = lax.broadcasted_iota(jnp.int32, (BS, BS), 1)
            block = block + jnp.where(across == along, rate_ref[0], 0.0)
        parts.append(split(block))
    left = (high_ref[0].reshape(KP * CB, BS), low_ref[0].reshape(KP * CB, BS))
    for k2 in range(PAIR):
        out_ref[k2, 0] = dot3(left, parts[k2])


def left_products(group, table, a_blocks, high, low, rates):
    half = pl.BlockSpec((1, KP, CB, BS), lambda s, t: (s, 0, 0, 0))
    return pl.pallas_call(
        functools.partial(left_kernel, group),
        grid_spec=pltpu.PrefetchScalarGridSpec(
            num_scalar_prefetch=1,
            grid=(NB,),
            in_specs=[
                pl.BlockSpec((1, PAIR, 1, BS, BS), lambda s, t: (s, 0, group, 0, 0)),
                half,
                half,
                pl.BlockSpec((1, 1, BS), lambda s, t: (t[NB * KA + s], 0, 0)),
            ],
            out_specs=pl.BlockSpec((PAIR, 1, KP * CB, BS), lambda s, t: (0, s, 0, 0)),
        ),
        out_shape=jax.ShapeDtypeStruct((PAIR, NB, KP * CB, BS), f32),
        cost_estimate=pl.CostEstimate(
            flops=NB * PAIR * 3 * 2 * BS**3,
            bytes_accessed=4 * PAIR * NB * 3 * BS * BS,
            transcendentals=0,
        ),
    )(table, a_blocks.reshape(NB, PAIR, GROUP, BS, BS), high, low, rates)


ROW_AT, SLOT_AT, PARITY_AT, HALF_AT, PICK_AT = 0, 16, 32, 34, 36


def product_kernel(table, t_ref, near_ref, far_ref, out_ref, p_high, p_low):
    m = pl.program_id(1)

    @pl.when(m == 0)
    def _():
        for k2, ref in enumerate((near_ref, far_ref)):
            ghost = jnp.concatenate(
                [ref[0, pl.ds(0, BS, KP), :], ref[0, pl.ds(1, BS, KP), :]], axis=1
            )
            high, low = split(ghost)
            p_high[k2] = high
            p_low[k2] = low

    for k2 in range(PAIR):
        result = dot3(split(t_ref[k2, 0]), (p_high[k2], p_low[k2]))
        half, parity = table[HALF_AT + k2], table[PARITY_AT + k2]
        out_ref[0, half, parity, 0] = result[:, :CB]
        out_ref[0, 1 - half, parity, 0] = result[:, CB:]


def products(table, left, near, far):
    source = lambda k2: pl.BlockSpec(
        (1, KP * BS, CB), lambda s, m, t: (t[PICK_AT + k2 * NB + s], 0, 0)
    )
    return pl.pallas_call(
        product_kernel,
        grid_spec=pltpu.PrefetchScalarGridSpec(
            num_scalar_prefetch=1,
            grid=(NB, KP),
            in_specs=[
                pl.BlockSpec((PAIR, 1, CB, BS), lambda s, m, t: (0, s, m, 0)),
                source(0),
                source(1),
            ],
            out_specs=pl.BlockSpec(
                (1, 2, 2, 1, CB, CB),
                lambda s, m, t: (t[ROW_AT + s * KP + m], 0, 0, t[SLOT_AT + s * KP + m], 0, 0),
            ),
            scratch_shapes=[pltpu.VMEM((PAIR, BS, BS), bf16)] * 2,
        ),
        out_shape=jax.ShapeDtypeStruct((N_ROW, 2, 2, 2, CB, CB), f32),
        cost_estimate=pl.CostEstimate(
            flops=NB * PAIR * 3 * 2 * BS**3,
            bytes_accessed=4 * PAIR * NB * 3 * BS * BS,
            transcendentals=0,
        ),
    )(table, left, near, far)


STEPS = 4
COUNT = 2 * N_ROW * N_X
PER_STEP = COUNT // STEPS
CELLS = N_X * N_ROW


def gather_kernel(group, table, got_ref, x_ref, *rest):
    coarse_ref, part_ref, floor_ref, total = rest[-4:]
    step = pl.program_id(0)

    @pl.when(step == 0)
    def _():
        total[...] = jnp.zeros_like(total)

    for b in range(PER_STEP):
        place = table[step * PER_STEP + b]
        total[place] += got_ref[b]

    @pl.when(step == STEPS - 1)
    def _():
        right = split(x_ref[...])
        for u in range(N_X):
            for q in range(N_ROW):
                coarse_ref[u, 0, pl.ds(q, CB, N_ROW), :] = total[u * N_ROW + q]
            row = jnp.concatenate([total[u * N_ROW + q] for q in range(N_ROW)], axis=1)
            part_ref[u, 0] = dot3(split(row), right)
        across = lax.broadcasted_iota(jnp.int32, (CB, CB), 0)
        along = lax.broadcasted_iota(jnp.int32, (CB, CB), 1)
        own = jnp.where(across == along, total[table[COUNT + 1]], 0.0)
        diag = jnp.maximum(jnp.abs(jnp.sum(own, axis=1, keepdims=True)), 1.0)
        floor_ref[...] = jnp.broadcast_to(diag, (CB, NCOL))


def gather(group, table, got, x, prior):
    whole = lambda shape: pl.BlockSpec(shape, lambda i, t: (0,) * len(shape))
    in_specs = [
        pl.BlockSpec((PER_STEP, CB, CB), lambda i, t: (i, 0, 0)),
        whole((N_ROW * CB, NCOL)),
    ]
    args = [got, x]
    alias = {}
    if prior is not None:
        in_specs += [pl.BlockSpec(memory_space=pl.ANY)] * 2
        args += prior
        alias = {3: 0, 4: 1}
    return pl.pallas_call(
        functools.partial(gather_kernel, group),
        grid_spec=pltpu.PrefetchScalarGridSpec(
            num_scalar_prefetch=1,
            grid=(STEPS,),
            in_specs=in_specs,
            out_specs=[
                pl.BlockSpec((N_X, 1, CB * N_ROW, CB), lambda i, t: (0, t[COUNT], 0, 0)),
                pl.BlockSpec((N_X, 1, CB, NCOL), lambda i, t: (0, t[COUNT], 0, 0)),
                whole((CB, NCOL)),
            ],
            scratch_shapes=[pltpu.VMEM((CELLS, CB, CB), f32)],
        ),
        out_shape=[
            jax.ShapeDtypeStruct((N_X, N_Y, CB * N_ROW, CB), f32),
            jax.ShapeDtypeStruct((N_X, N_Y, CB, NCOL), f32),
            jax.ShapeDtypeStruct((CB, NCOL), f32),
        ],
        input_output_aliases=alias,
        cost_estimate=pl.CostEstimate(
            flops=3 * 2 * N_X * CB * N_ROW * CB * NCOL,
            bytes_accessed=4 * (COUNT + CELLS + 2 * CELLS) * CB * CB,
            transcendentals=0,
        ),
    )(table, *args)


def apply_kernel(c_ref, x_ref, out_ref, x_high, x_low):
    @pl.when(pl.program_id(0) == 0)
    def _():
        high, low = split(x_ref[...])
        x_high[...] = high
        x_low[...] = low

    row = jnp.concatenate([c_ref[pl.ds(q, CB, N_ROW), :] for q in range(N_ROW)], axis=1)
    out_ref[...] = dot3(split(row), (x_high[...], x_low[...]))


def apply(coarse, x):
    return pl.pallas_call(
        apply_kernel,
        grid=(N_COL,),
        in_specs=[
            pl.BlockSpec((CB * N_ROW, CB), lambda u: (u, 0)),
            pl.BlockSpec((N_ROW * CB, NCOL), lambda u: (0, 0)),
        ],
        out_specs=pl.BlockSpec((CB, NCOL), lambda u: (u, 0)),
        out_shape=jax.ShapeDtypeStruct((N_COL * CB, NCOL), f32),
        scratch_shapes=[pltpu.VMEM((N_ROW * CB, NCOL), bf16)] * 2,
    )(coarse, x)


def to_all(value, axes, count):
    copies = jnp.broadcast_to(value[None], (count,) + value.shape)
    return lax.all_to_all(copies, axes, split_axis=0, concat_axis=0, tiled=True)


def places(metas, row, col):
    delta = jnp.arange(N_COL, dtype=jnp.int32)
    p_cols = metas[:, :, :, :KP]
    entries = p_cols.reshape(N_ROW, N_COL, NB * KP)
    match = (entries // N_COL == row).astype(jnp.int32)
    earlier = jnp.cumsum(match, axis=2) - match
    order = jnp.arange(NB * KP, dtype=jnp.int32)
    sources = [
        lax.dynamic_index_in_dim(metas, (col + h * KA) % N_COL, 1, False) for h in range(2)
    ]
    result = []
    for t in range(2):
        chosen = match * (earlier == t)
        entry = jnp.sum(chosen * order, axis=2)
        u = jnp.sum(chosen * (entries % N_COL), axis=2)
        block = entry // KP
        far = (delta - col) % N_COL
        k, half = far % KA, far // KA
        quotient = jnp.zeros_like(u)
        for h in range(2):
            cells = sources[h]
            identity = jnp.broadcast_to(jnp.arange(NB, dtype=jnp.int32)[None, :, None], (N_ROW, NB, 1))
            picks = jnp.concatenate([identity, cells[:, :, KP:]], axis=2)
            hit = (block[:, :, None, None] == jnp.arange(NB)[None, None, :, None]) & (
                k[None, :, None, None] == jnp.arange(KA)[None, None, None, :]
            )
            pick = jnp.sum(jnp.where(hit, picks[:, None], 0), axis=(2, 3))
            value = jnp.sum(
                jnp.where(pick[:, :, None] == jnp.arange(NB), cells[:, None, :, h] // N_COL, 0), axis=2
            )
            quotient = jnp.where(half[None, :] == h, value, quotient)
        result.append(u * N_ROW + quotient)
    return jnp.stack(result, axis=2).reshape(-1)


def shifted(value, axis, steps):
    count = lax.axis_size(axis)
    return lax.ppermute(value, axis, [(i, (i + steps) % count) for i in range(count)])


def exchanged(value, axes):
    return lax.all_to_all(value, axes, split_axis=0, concat_axis=0, tiled=True)


def product_table(metas, group, row, x, y):
    mine = lax.dynamic_index_in_dim(metas, row, 0, False)
    source = lax.dynamic_index_in_dim(mine, x * N_Y + (y + group) % N_Y, 0, False)
    entry_row = (source[:, :KP] // N_COL).reshape(-1)
    order = jnp.arange(NB * KP, dtype=jnp.int32)
    slot = jnp.sum(
        (entry_row[None, :] == entry_row[:, None]) & (order[None, :] < order[:, None]),
        axis=1,
        dtype=jnp.int32,
    )
    back = (y + group) // N_Y
    targets, picks = [], []
    for k2 in range(PAIR):
        k = group + GROUP * k2
        e_x = (x - back - k2) % N_X
        targets.append(e_x)
        if k == 0:
            pick = jnp.arange(NB, dtype=jnp.int32)
        else:
            cells = lax.dynamic_index_in_dim(mine, e_x * N_Y + y, 0, False)
            pick = cells[:, KP + k - 1]
        picks.append(pick if group == 0 else pick + (back + k2) * NB)
    target = jnp.stack(targets)
    return jnp.concatenate([entry_row, slot, target % 2, target // 2] + picks)


def on_device(a_blocks, a_live, p_blocks, p_cols, ghost_list, policy, rates, rhs, guess):
    x = lax.axis_index("x")
    y = lax.axis_index("y")
    row = lax.axis_index(ROW)
    col = x * N_Y + y
    own_p = p_blocks.reshape(NB, BS * KP, CB)
    p_one = shifted(own_p, "x", 1)
    p_two = shifted(own_p, "x", 2)
    meta = jnp.concatenate([p_cols, ghost_list], axis=1)
    metas = to_all(meta.reshape(-1), ALL, DEV).reshape(N_ROW, N_COL, NB, KP + KA - 1)
    around = to_all(guess, ROW, N_ROW).reshape(N_ROW * CB, NCOL)

    high, low = transposed(own_p)
    numbers = jnp.concatenate([a_live.reshape(-1), policy])
    rate_rows = rates.reshape(-1, 1, BS)
    lefts = {}
    for group in (1, 3, 2, 0):
        left = left_products(group, numbers, a_blocks, high, low, rate_rows)
        lefts[group] = shifted(left, "y", -group) if group else left

    where = places(metas, row, col).reshape(N_ROW, N_X, N_Y, 2)
    where = where // (N_Y * N_ROW) * N_ROW + where % N_ROW
    own_cell = x * N_ROW + row
    prior = None
    stacked = None
    for group in (0, 1, 3, 2):
        table = product_table(metas, group, row, x, y)
        if group == 0:
            sent = products(table, lefts[group], own_p, p_one)
        else:
            if stacked is None:
                stacked = jnp.concatenate([own_p, p_one, p_two])
            sent = products(table, lefts[group], stacked, stacked)
        got = exchanged(sent.reshape(N_ROW * N_X, 2, CB, CB), PLANE).reshape(COUNT, CB, CB)
        y_u = (y + group) % N_Y
        spots = lax.dynamic_index_in_dim(where, y_u, 2, False).reshape(-1)
        spots = jnp.concatenate([spots, jnp.stack([y_u, own_cell])])
        coarse, part, floor = gather(group, spots, got, around, prior)
        if group == 0:
            floor_diag = floor
        prior = [coarse, part]
    coarse = coarse.reshape(N_COL * CB * N_ROW, CB)
    current = guess
    for sweep in range(2):
        if sweep:
            part = apply(coarse, to_all(current, ROW, N_ROW).reshape(N_ROW * CB, NCOL))
        pieces = exchanged(part.reshape(N_COL, CB, NCOL), COL)
        applied = jnp.sum(pieces, axis=0)
        current = current + damping * (rhs - applied) / floor_diag
    return coarse.reshape(N_COL * CB, N_ROW, 1, CB), current


def solution(mesh):
    mesh = Mesh(mesh.devices.reshape(N_ROW // 2, 2, N_X, N_Y), ALL)
    return jax.shard_map(
        on_device,
        mesh=mesh,
        in_specs=(
            P(ALL, None, None, None),
            P(ALL, None),
            P(ALL, None, None, None),
            P(ALL, None),
            P(ALL, None),
            P(ALL),
            P(),
            P(ALL, None),
            P(ALL, None),
        ),
        out_specs=(P(ROW, None, COL, None), P(ALL, None)),
        check_vma=False,
    )
```

```python
import functools

import jax
import jax.numpy as jnp
from jax import lax
from jax.experimental import pallas as pl
from jax.experimental.pallas import tpu as pltpu
from jax.sharding import Mesh, PartitionSpec as P

BS = 256
CB = 128
KA = 8
KP = 2
N_ROW = 8
N_COL = 16
NB = 8
NCOL = 256
damping = 0.7
f32 = jnp.float32
bf16 = jnp.bfloat16
ROW = ("z", "core")
COL = ("x", "y")
ALL = ROW + COL
PLANE = ROW + ("x",)
N_X = N_Y = 4
GROUP = 4
PAIR = 2


def split(value):
    high = value.astype(bf16)
    return high, (value - high.astype(f32)).astype(bf16)


def dot3(lhs, rhs):
    left = jnp.concatenate([lhs[0], lhs[0], lhs[1]], axis=1)
    right = jnp.concatenate([rhs[0], rhs[1], rhs[0]], axis=0)
    return jnp.dot(left, right, preferred_element_type=f32)


def transpose_kernel(p_ref, high_ref, low_ref):
    for m in range(KP):
        high, low = split(p_ref[0, pl.ds(m, BS, KP), :].T)
        high_ref[0, m] = high
        low_ref[0, m] = low


def transposed(own_p):
    shape = jax.ShapeDtypeStruct((NB, KP, CB, BS), bf16)
    spec = pl.BlockSpec((1, KP, CB, BS), lambda s: (s, 0, 0, 0))
    return pl.pallas_call(
        transpose_kernel,
        grid=(NB,),
        in_specs=[pl.BlockSpec((1, KP * BS, CB), lambda s: (s, 0, 0))],
        out_specs=[spec, spec],
        out_shape=[shape, shape],
    )(own_p)


def left_kernel(group, table, a_ref, high_ref, low_ref, rate_ref, out_ref):
    s = pl.program_id(0)
    parts = []
    for k2 in range(PAIR):
        block = a_ref[0, k2, 0] * table[s * KA + group + GROUP * k2].astype(f32)
        if group == 0 and k2 == 0:
            across = lax.broadcasted_iota(jnp.int32, (BS, BS), 0)
            along = lax.broadcasted_iota(jnp.int32, (BS, BS), 1)
            block = block + jnp.where(across == along, rate_ref[0], 0.0)
        parts.append(split(block))
    left = (high_ref[0].reshape(KP * CB, BS), low_ref[0].reshape(KP * CB, BS))
    for k2 in range(PAIR):
        out_ref[k2, 0] = dot3(left, parts[k2])


def left_products(group, table, a_blocks, high, low, rates):
    half = pl.BlockSpec((1, KP, CB, BS), lambda s, t: (s, 0, 0, 0))
    return pl.pallas_call(
        functools.partial(left_kernel, group),
        grid_spec=pltpu.PrefetchScalarGridSpec(
            num_scalar_prefetch=1,
            grid=(NB,),
            in_specs=[
                pl.BlockSpec((1, PAIR, 1, BS, BS), lambda s, t: (s, 0, group, 0, 0)),
                half,
                half,
                pl.BlockSpec((1, 1, BS), lambda s, t: (t[NB * KA + s], 0, 0)),
            ],
            out_specs=pl.BlockSpec((PAIR, 1, KP * CB, BS), lambda s, t: (0, s, 0, 0)),
        ),
        out_shape=jax.ShapeDtypeStruct((PAIR, NB, KP * CB, BS), f32),
        cost_estimate=pl.CostEstimate(
            flops=NB * PAIR * 3 * 2 * BS**3,
            bytes_accessed=4 * PAIR * NB * 3 * BS * BS,
            transcendentals=0,
        ),
    )(table, a_blocks.reshape(NB, PAIR, GROUP, BS, BS), high, low, rates)


ROW_AT, SLOT_AT, PARITY_AT, HALF_AT, PICK_AT, TABLE = 0, 16, 32, 34, 36, 52


def product_kernel(base, table, t_ref, near_ref, far_ref, out_ref, held, sems):
    s = pl.program_id(0)
    now = lax.rem(s, 2)

    def copy(step, m):
        return pltpu.make_async_copy(
            held.at[lax.rem(step, 2), m],
            out_ref.at[
                table[base + ROW_AT + step * KP + m], :, :, table[base + SLOT_AT + step * KP + m]
            ],
            sems.at[lax.rem(step, 2), m],
        )

    @pl.when(s >= 2)
    def _():
        for m in range(KP):
            copy(s - 2, m).wait()

    for k2, ref in enumerate((near_ref, far_ref)):
        ghost = jnp.concatenate(
            [ref[0, pl.ds(0, BS, KP), :], ref[0, pl.ds(1, BS, KP), :]], axis=1
        )
        result = dot3(split(t_ref[k2, 0]), split(ghost))
        half, parity = table[base + HALF_AT + k2], table[base + PARITY_AT + k2]
        for m in range(KP):
            held[now, m, half, parity] = result[m * CB : (m + 1) * CB, :CB]
            held[now, m, 1 - half, parity] = result[m * CB : (m + 1) * CB, CB:]
    for m in range(KP):
        copy(s, m).start()

    @pl.when(s == NB - 1)
    def _():
        for step in (NB - 2, NB - 1):
            for m in range(KP):
                copy(step, m).wait()


def products(group, table, left, near, far):
    base = group * TABLE
    source = lambda k2: pl.BlockSpec(
        (1, KP * BS, CB), lambda s, t: (t[base + PICK_AT + k2 * NB + s], 0, 0)
    )
    return pl.pallas_call(
        functools.partial(product_kernel, base),
        grid_spec=pltpu.PrefetchScalarGridSpec(
            num_scalar_prefetch=1,
            grid=(NB,),
            in_specs=[
                pl.BlockSpec((PAIR, 1, KP * CB, BS), lambda s, t: (0, s, 0, 0)),
                source(0),
                source(1),
            ],
            out_specs=pl.BlockSpec(memory_space=pl.ANY),
            scratch_shapes=[
                pltpu.VMEM((2, KP, 2, 2, CB, CB), f32),
                pltpu.SemaphoreType.DMA((2, KP)),
            ],
        ),
        out_shape=jax.ShapeDtypeStruct((N_ROW, 2, 2, 2, CB, CB), f32),
        cost_estimate=pl.CostEstimate(
            flops=NB * PAIR * 3 * 2 * BS**3,
            bytes_accessed=4 * PAIR * NB * 3 * BS * BS,
            transcendentals=0,
        ),
    )(table, left, near, far)


STEPS = 4
COUNT = 2 * N_ROW * N_X
PER_STEP = COUNT // STEPS
CELLS = N_X * N_ROW


def gather_kernel(group, table, got_ref, x_ref, *rest):
    coarse_ref, part_ref, floor_ref, total, x_high, x_low = rest[-6:]
    step = pl.program_id(0)

    @pl.when(step == 0)
    def _():
        total[...] = jnp.zeros_like(total)
        high, low = split(x_ref[...])
        x_high[...] = high
        x_low[...] = low

    for b in range(PER_STEP):
        place = table[step * PER_STEP + b]
        total[place] += got_ref[b]

    @pl.when(step == STEPS - 1)
    def _():
        rows = []
        for u in range(N_X):
            for q in range(N_ROW):
                coarse_ref[u, 0, pl.ds(q, CB, N_ROW), :] = total[u * N_ROW + q]
            rows.append(jnp.concatenate([total[u * N_ROW + q] for q in range(N_ROW)], axis=1))
        result = dot3(split(jnp.concatenate(rows)), (x_high[...], x_low[...]))
        for u in range(N_X):
            part_ref[u, 0] = result[u * CB : (u + 1) * CB]
        if group == 0:
            across = lax.broadcasted_iota(jnp.int32, (CB, CB), 0)
            along = lax.broadcasted_iota(jnp.int32, (CB, CB), 1)
            own = jnp.where(across == along, total[table[COUNT + 1]], 0.0)
            diag = jnp.maximum(jnp.abs(jnp.sum(own, axis=1, keepdims=True)), 1.0)
            floor_ref[...] = jnp.broadcast_to(diag, (CB, NCOL))


def gather(group, table, got, x, prior):
    whole = lambda shape: pl.BlockSpec(shape, lambda i, t: (0,) * len(shape))
    in_specs = [
        pl.BlockSpec((PER_STEP, CB, CB), lambda i, t: (i, 0, 0)),
        whole((N_ROW * CB, NCOL)),
    ]
    args = [got, x]
    alias = {}
    if prior is not None:
        in_specs += [pl.BlockSpec(memory_space=pl.ANY)] * 2
        args += prior
        alias = {3: 0, 4: 1}
    return pl.pallas_call(
        functools.partial(gather_kernel, group),
        grid_spec=pltpu.PrefetchScalarGridSpec(
            num_scalar_prefetch=1,
            grid=(STEPS,),
            in_specs=in_specs,
            out_specs=[
                pl.BlockSpec((N_X, 1, CB * N_ROW, CB), lambda i, t: (0, t[COUNT], 0, 0)),
                pl.BlockSpec((N_X, 1, CB, NCOL), lambda i, t: (0, t[COUNT], 0, 0)),
                whole((CB, NCOL)),
            ],
            scratch_shapes=[
                pltpu.VMEM((CELLS, CB, CB), f32),
                pltpu.VMEM((N_ROW * CB, NCOL), bf16),
                pltpu.VMEM((N_ROW * CB, NCOL), bf16),
            ],
        ),
        out_shape=[
            jax.ShapeDtypeStruct((N_X, N_Y, CB * N_ROW, CB), f32),
            jax.ShapeDtypeStruct((N_X, N_Y, CB, NCOL), f32),
            jax.ShapeDtypeStruct((CB, NCOL), f32),
        ],
        input_output_aliases=alias,
        cost_estimate=pl.CostEstimate(
            flops=3 * 2 * N_X * CB * N_ROW * CB * NCOL,
            bytes_accessed=4 * (COUNT + CELLS + 2 * CELLS) * CB * CB,
            transcendentals=0,
        ),
    )(table, *args)


TALL = 4 * CB


def apply_kernel(c_ref, x_ref, out_ref, x_high, x_low):
    @pl.when(pl.program_id(0) == 0)
    def _():
        high, low = split(x_ref[...])
        x_high[...] = high
        x_low[...] = low

    rows = jnp.concatenate([c_ref[pl.ds(q, TALL, N_ROW), :] for q in range(N_ROW)], axis=1)
    out_ref[...] = dot3(split(rows), (x_high[...], x_low[...]))


def apply(coarse, x):
    return pl.pallas_call(
        apply_kernel,
        grid=(N_COL * CB // TALL,),
        in_specs=[
            pl.BlockSpec((TALL * N_ROW, CB), lambda u: (u, 0)),
            pl.BlockSpec((N_ROW * CB, NCOL), lambda u: (0, 0)),
        ],
        out_specs=pl.BlockSpec((TALL, NCOL), lambda u: (u, 0)),
        out_shape=jax.ShapeDtypeStruct((N_COL * CB, NCOL), f32),
        scratch_shapes=[pltpu.VMEM((N_ROW * CB, NCOL), bf16)] * 2,
    )(coarse, x)


def to_all(value, axes, count):
    copies = jnp.broadcast_to(value[None], (count,) + value.shape)
    return lax.all_to_all(copies, axes, split_axis=0, concat_axis=0, tiled=True)


def places(metas, row, col):
    delta = jnp.arange(N_COL, dtype=jnp.int32)
    p_cols = metas[:, :, :, :KP]
    entries = p_cols.reshape(N_ROW, N_COL, NB * KP)
    match = (entries // N_COL == row).astype(jnp.int32)
    earlier = jnp.cumsum(match, axis=2) - match
    order = jnp.arange(NB * KP, dtype=jnp.int32)
    sources = [
        lax.dynamic_index_in_dim(metas, (col + h * KA) % N_COL, 1, False) for h in range(2)
    ]
    result = []
    for t in range(2):
        chosen = match * (earlier == t)
        entry = jnp.sum(chosen * order, axis=2)
        u = jnp.sum(chosen * (entries % N_COL), axis=2)
        block = entry // KP
        far = (delta - col) % N_COL
        k, half = far % KA, far // KA
        quotient = jnp.zeros_like(u)
        for h in range(2):
            cells = sources[h]
            identity = jnp.broadcast_to(jnp.arange(NB, dtype=jnp.int32)[None, :, None], (N_ROW, NB, 1))
            picks = jnp.concatenate([identity, cells[:, :, KP:]], axis=2)
            hit = (block[:, :, None, None] == jnp.arange(NB)[None, None, :, None]) & (
                k[None, :, None, None] == jnp.arange(KA)[None, None, None, :]
            )
            pick = jnp.sum(jnp.where(hit, picks[:, None], 0), axis=(2, 3))
            value = jnp.sum(
                jnp.where(pick[:, :, None] == jnp.arange(NB), cells[:, None, :, h] // N_COL, 0), axis=2
            )
            quotient = jnp.where(half[None, :] == h, value, quotient)
        result.append(u * N_ROW + quotient)
    return jnp.stack(result, axis=2).reshape(-1)


def shifted(value, axis, steps):
    count = lax.axis_size(axis)
    return lax.ppermute(value, axis, [(i, (i + steps) % count) for i in range(count)])


def exchanged(value, axes):
    return lax.all_to_all(value, axes, split_axis=0, concat_axis=0, tiled=True)


META = KP + KA - 1


def product_tables(cells, x, y):
    groups = jnp.arange(GROUP, dtype=jnp.int32)
    columns = [x * N_Y + (y + groups) % N_Y]
    back = (y + groups) // N_Y
    e_x = jnp.stack([(x - back - k2) % N_X for k2 in range(PAIR)])
    columns.append((e_x * N_Y + y).reshape(-1))
    wanted = jnp.concatenate(columns)
    chosen = (wanted[:, None] == jnp.arange(N_COL, dtype=jnp.int32)[None, :]).astype(f32)
    found = jnp.dot(chosen, cells, precision=lax.Precision.HIGHEST)
    found = (found + 0.5).astype(jnp.int32).reshape(-1, NB, META)
    entry_row = (found[:GROUP, :, :KP] // N_COL).reshape(GROUP, NB * KP)
    order = jnp.arange(NB * KP, dtype=jnp.int32)
    slot = jnp.sum(
        (entry_row[:, None, :] == entry_row[:, :, None]) & (order[None, None, :] < order[None, :, None]),
        axis=2,
        dtype=jnp.int32,
    )
    picks = [jnp.arange(NB, dtype=jnp.int32)]
    for k in range(1, KA):
        picks.append(found[GROUP + k, :, KP + k - 1])
    picks = jnp.stack(picks).reshape(PAIR, GROUP, NB)
    offset = jnp.where(groups == 0, 0, (back[None, :] + jnp.arange(PAIR)[:, None]) * NB)
    picks = (picks + offset[:, :, None]).transpose(1, 0, 2).reshape(GROUP, PAIR * NB)
    return jnp.concatenate([entry_row, slot, e_x.T % 2, e_x.T // 2, picks], axis=1).reshape(-1)


def on_device(a_blocks, a_live, p_blocks, p_cols, ghost_list, policy, rates, rhs, guess):
    x = lax.axis_index("x")
    y = lax.axis_index("y")
    row = lax.axis_index(ROW)
    col = x * N_Y + y
    own_p = p_blocks.reshape(NB, BS * KP, CB)
    p_one = shifted(own_p, "x", 1)
    meta = jnp.concatenate([p_cols, ghost_list], axis=1).astype(f32).reshape(-1)
    cells = to_all(meta, COL, N_COL)
    spare = -(-N_COL * NB * META // NCOL)
    spare = -(-spare // 8) * 8
    padded = jnp.pad(cells.reshape(-1), (0, spare * NCOL - cells.size)).reshape(spare, NCOL)
    packed = to_all(jnp.concatenate([guess, padded]), ROW, N_ROW)
    around = packed[:, :CB].reshape(N_ROW * CB, NCOL)
    metas = packed[:, CB:].reshape(N_ROW, spare * NCOL)[:, : cells.size]
    metas = (metas + 0.5).astype(jnp.int32).reshape(N_ROW, N_COL, NB, META)

    high, low = transposed(own_p)
    numbers = jnp.concatenate([a_live.reshape(-1), policy])
    rate_rows = rates.reshape(-1, 1, BS)
    lefts = {}
    for group in (1, 3, 2, 0):
        left = left_products(group, numbers, a_blocks, high, low, rate_rows)
        lefts[group] = shifted(left, "y", -group) if group else left
    p_two = shifted(p_one, "x", 1)

    table = product_tables(cells, x, y)
    where = places(metas, row, col).reshape(N_ROW, N_X, N_Y, 2)
    where = where // (N_Y * N_ROW) * N_ROW + where % N_ROW
    own_cell = x * N_ROW + row
    prior = None
    stacked = None
    for group in (0, 1, 3, 2):
        near, far = own_p, p_one
        if group:
            if stacked is None:
                stacked = jnp.concatenate([own_p, p_one, p_two])
            near = far = stacked
        sent = products(group, table, lefts[group], near, far)
        got = exchanged(sent.reshape(N_ROW * N_X, 2, CB, CB), PLANE)
        y_u = (y + group) % N_Y
        spots = lax.dynamic_index_in_dim(where, y_u, 2, False).reshape(-1)
        spots = jnp.concatenate([spots, jnp.stack([y_u, own_cell])])
        coarse, part, floor = gather(group, spots, got.reshape(COUNT, CB, CB), around, prior)
        if group == 0:
            floor_diag = floor
        prior = [coarse, part]
    coarse = coarse.reshape(N_COL * CB * N_ROW, CB)
    current = guess
    for sweep in range(2):
        if sweep:
            part = apply(coarse, to_all(current, ROW, N_ROW).reshape(N_ROW * CB, NCOL))
        pieces = exchanged(part.reshape(N_COL, CB, NCOL), COL)
        applied = jnp.sum(pieces, axis=0)
        current = current + damping * (rhs - applied) / floor_diag
    return coarse.reshape(N_COL * CB, N_ROW, 1, CB), current


def solution(mesh):
    mesh = Mesh(mesh.devices.reshape(N_ROW // 2, 2, N_X, N_Y), ALL)

    return jax.shard_map(
        on_device,
        mesh=mesh,
        in_specs=(
            P(ALL, None, None, None),
            P(ALL, None),
            P(ALL, None, None, None),
            P(ALL, None),
            P(ALL, None),
            P(ALL),
            P(),
            P(ALL, None),
            P(ALL, None),
        ),
        out_specs=(P(ROW, None, COL, None), P(ALL, None)),
        check_vma=False,
    )
```

```python
import functools

import jax
import jax.numpy as jnp
from jax import lax
from jax.experimental import pallas as pl
from jax.experimental.pallas import tpu as pltpu
from jax.sharding import Mesh, PartitionSpec as P

BS = 256
CB = 128
KA = 8
KP = 2
N_ROW = 8
N_COL = 16
NB = 8
NCOL = 256
damping = 0.7
f32 = jnp.float32
bf16 = jnp.bfloat16
ROW = ("z", "core")
COL = ("x", "y")
ALL = ROW + COL
PLANE = ROW + ("x",)
N_X = N_Y = 4
GROUP = 4
PAIR = 2


def split(value):
    high = value.astype(bf16)
    return high, (value - high.astype(f32)).astype(bf16)


def dot3(lhs, rhs):
    left = jnp.concatenate([lhs[0], lhs[0], lhs[1]], axis=1)
    right = jnp.concatenate([rhs[0], rhs[1], rhs[0]], axis=0)
    return jnp.dot(left, right, preferred_element_type=f32)


STEP = 2


def left_kernel(group, flips, table, a_ref, rate_a, rate_b, *rest):
    if flips:
        p_ref, out_ref, high_ref, low_ref = rest
    else:
        high_ref, low_ref, out_ref = rest
    step = pl.program_id(0)
    for r, rate_ref in enumerate((rate_a, rate_b)):
        s = step * STEP + r
        if flips:
            for m in range(KP):
                high, low = split(p_ref[r, pl.ds(m, BS, KP), :].T)
                high_ref[r, m * CB : (m + 1) * CB] = high
                low_ref[r, m * CB : (m + 1) * CB] = low
        for k2 in range(PAIR):
            block = a_ref[r, k2, 0] * table[s * KA + group + GROUP * k2].astype(f32)
            if group == 0 and k2 == 0:
                across = lax.broadcasted_iota(jnp.int32, (BS, BS), 0)
                along = lax.broadcasted_iota(jnp.int32, (BS, BS), 1)
                block = block + jnp.where(across == along, rate_ref[0], 0.0)
            out_ref[k2, r] = dot3((high_ref[r], low_ref[r]), split(block))


def left_products(group, table, a_blocks, rates, own_p, parts):
    half = pl.BlockSpec((STEP, KP * CB, BS), lambda s, t: (s, 0, 0))
    halves = [jax.ShapeDtypeStruct((NB, KP * CB, BS), bf16)] * 2
    flips = parts is None
    rate = lambda r: pl.BlockSpec((1, 1, BS), lambda s, t: (t[NB * KA + s * STEP + r], 0, 0))
    results = pl.pallas_call(
        functools.partial(left_kernel, group, flips),
        grid_spec=pltpu.PrefetchScalarGridSpec(
            num_scalar_prefetch=1,
            grid=(NB // STEP,),
            in_specs=[
                pl.BlockSpec((STEP, PAIR, 1, BS, BS), lambda s, t: (s, 0, group, 0, 0)),
                rate(0),
                rate(1),
            ]
            + ([pl.BlockSpec((STEP, KP * BS, CB), lambda s, t: (s, 0, 0))] if flips else [half, half]),
            out_specs=[pl.BlockSpec((PAIR, STEP, KP * CB, BS), lambda s, t: (0, s, 0, 0))]
            + ([half, half] if flips else []),
        ),
        out_shape=[jax.ShapeDtypeStruct((PAIR, NB, KP * CB, BS), f32)] + (halves if flips else []),
        cost_estimate=pl.CostEstimate(
            flops=NB * PAIR * 3 * 2 * BS**3,
            bytes_accessed=4 * PAIR * NB * 3 * BS * BS,
            transcendentals=0,
        ),
    )(table, a_blocks.reshape(NB, PAIR, GROUP, BS, BS), rates, rates, *([own_p] if flips else parts))
    return results[0], (list(results[1:]) if flips else parts)


ROW_AT, SLOT_AT, PARITY_AT, HALF_AT, PICK_AT, TABLE = 0, 16, 32, 34, 36, 52


def product_kernel(base, table, t_ref, *rest):
    sources, (out_ref, held, sems) = rest[: PAIR * STEP], rest[PAIR * STEP :]
    step = pl.program_id(0)

    def copy(step, r, m):
        entry = (step * STEP + r) * KP + m
        return pltpu.make_async_copy(
            held.at[lax.rem(step, 2), r, m],
            out_ref.at[table[base + ROW_AT + entry], :, :, table[base + SLOT_AT + entry]],
            sems.at[lax.rem(step, 2), r, m],
        )

    def each(step, act):
        for r in range(STEP):
            for m in range(KP):
                act(copy(step, r, m))

    @pl.when(step >= 2)
    def _():
        each(step - 2, lambda c: c.wait())

    now = lax.rem(step, 2)
    for r in range(STEP):
        for k2 in range(PAIR):
            ref = sources[r * PAIR + k2]
            ghost = jnp.concatenate(
                [ref[0, pl.ds(0, BS, KP), :], ref[0, pl.ds(1, BS, KP), :]], axis=1
            )
            result = dot3(split(t_ref[k2, r]), split(ghost))
            half, parity = table[base + HALF_AT + k2], table[base + PARITY_AT + k2]
            for m in range(KP):
                held[now, r, m, half, parity] = result[m * CB : (m + 1) * CB, :CB]
                held[now, r, m, 1 - half, parity] = result[m * CB : (m + 1) * CB, CB:]
    each(step, lambda c: c.start())

    @pl.when(step == NB // STEP - 1)
    def _():
        each(NB // STEP - 2, lambda c: c.wait())
        each(NB // STEP - 1, lambda c: c.wait())


def products(group, table, left, near, far):
    base = group * TABLE
    source = lambda r, k2: pl.BlockSpec(
        (1, KP * BS, CB), lambda s, t: (t[base + PICK_AT + k2 * NB + s * STEP + r], 0, 0)
    )
    return pl.pallas_call(
        functools.partial(product_kernel, base),
        grid_spec=pltpu.PrefetchScalarGridSpec(
            num_scalar_prefetch=1,
            grid=(NB // STEP,),
            in_specs=[pl.BlockSpec((PAIR, STEP, KP * CB, BS), lambda s, t: (0, s, 0, 0))]
            + [source(r, k2) for r in range(STEP) for k2 in range(PAIR)],
            out_specs=pl.BlockSpec(memory_space=pl.ANY),
            scratch_shapes=[
                pltpu.VMEM((2, STEP, KP, 2, 2, CB, CB), f32),
                pltpu.SemaphoreType.DMA((2, STEP, KP)),
            ],
        ),
        out_shape=jax.ShapeDtypeStruct((N_ROW, 2, 2, 2, CB, CB), f32),
        cost_estimate=pl.CostEstimate(
            flops=NB * PAIR * 3 * 2 * BS**3,
            bytes_accessed=4 * PAIR * NB * 3 * BS * BS,
            transcendentals=0,
        ),
    )(table, left, *[near, far] * STEP)


STEPS = 4
COUNT = 2 * N_ROW * N_X
PER_STEP = COUNT // STEPS
CELLS = N_X * N_ROW


def gather_kernel(group, table, got_ref, x_ref, *rest):
    coarse_ref, part_ref, floor_ref, total, x_high, x_low = rest[-6:]
    step = pl.program_id(0)

    @pl.when(step == 0)
    def _():
        total[...] = jnp.zeros_like(total)
        high, low = split(x_ref[...])
        x_high[...] = high
        x_low[...] = low

    for b in range(PER_STEP):
        place = table[step * PER_STEP + b]
        total[place] += got_ref[b]

    @pl.when(step == STEPS - 1)
    def _():
        rows = []
        for u in range(N_X):
            for q in range(N_ROW):
                coarse_ref[u, 0, pl.ds(q, CB, N_ROW), :] = total[u * N_ROW + q]
            rows.append(jnp.concatenate([total[u * N_ROW + q] for q in range(N_ROW)], axis=1))
        result = dot3(split(jnp.concatenate(rows)), (x_high[...], x_low[...]))
        for u in range(N_X):
            part_ref[u, 0] = result[u * CB : (u + 1) * CB]
        if group == 0:
            across = lax.broadcasted_iota(jnp.int32, (CB, CB), 0)
            along = lax.broadcasted_iota(jnp.int32, (CB, CB), 1)
            own = jnp.where(across == along, total[table[COUNT + 1]], 0.0)
            diag = jnp.maximum(jnp.abs(jnp.sum(own, axis=1, keepdims=True)), 1.0)
            floor_ref[...] = jnp.broadcast_to(diag, (CB, NCOL))


def gather(group, table, got, x, prior):
    whole = lambda shape: pl.BlockSpec(shape, lambda i, t: (0,) * len(shape))
    in_specs = [
        pl.BlockSpec((PER_STEP, CB, CB), lambda i, t: (i, 0, 0)),
        whole((N_ROW * CB, NCOL)),
    ]
    args = [got, x]
    alias = {}
    if prior is not None:
        in_specs += [pl.BlockSpec(memory_space=pl.ANY)] * 2
        args += prior
        alias = {3: 0, 4: 1}
    return pl.pallas_call(
        functools.partial(gather_kernel, group),
        grid_spec=pltpu.PrefetchScalarGridSpec(
            num_scalar_prefetch=1,
            grid=(STEPS,),
            in_specs=in_specs,
            out_specs=[
                pl.BlockSpec((N_X, 1, CB * N_ROW, CB), lambda i, t: (0, t[COUNT], 0, 0)),
                pl.BlockSpec((N_X, 1, CB, NCOL), lambda i, t: (0, t[COUNT], 0, 0)),
                whole((CB, NCOL)),
            ],
            scratch_shapes=[
                pltpu.VMEM((CELLS, CB, CB), f32),
                pltpu.VMEM((N_ROW * CB, NCOL), bf16),
                pltpu.VMEM((N_ROW * CB, NCOL), bf16),
            ],
        ),
        out_shape=[
            jax.ShapeDtypeStruct((N_X, N_Y, CB * N_ROW, CB), f32),
            jax.ShapeDtypeStruct((N_X, N_Y, CB, NCOL), f32),
            jax.ShapeDtypeStruct((CB, NCOL), f32),
        ],
        input_output_aliases=alias,
        cost_estimate=pl.CostEstimate(
            flops=3 * 2 * N_X * CB * N_ROW * CB * NCOL,
            bytes_accessed=4 * (COUNT + CELLS + 2 * CELLS) * CB * CB,
            transcendentals=0,
        ),
    )(table, *args)


TALL = 4 * CB


def apply_kernel(c_ref, x_ref, out_ref, x_high, x_low):
    @pl.when(pl.program_id(0) == 0)
    def _():
        high, low = split(x_ref[...])
        x_high[...] = high
        x_low[...] = low

    rows = jnp.concatenate([c_ref[pl.ds(q, TALL, N_ROW), :] for q in range(N_ROW)], axis=1)
    out_ref[...] = dot3(split(rows), (x_high[...], x_low[...]))


def apply(coarse, x):
    return pl.pallas_call(
        apply_kernel,
        grid=(N_COL * CB // TALL,),
        in_specs=[
            pl.BlockSpec((TALL * N_ROW, CB), lambda u: (u, 0)),
            pl.BlockSpec((N_ROW * CB, NCOL), lambda u: (0, 0)),
        ],
        out_specs=pl.BlockSpec((TALL, NCOL), lambda u: (u, 0)),
        out_shape=jax.ShapeDtypeStruct((N_COL * CB, NCOL), f32),
        scratch_shapes=[pltpu.VMEM((N_ROW * CB, NCOL), bf16)] * 2,
    )(coarse, x)


def to_all(value, axes, count):
    copies = jnp.broadcast_to(value[None], (count,) + value.shape)
    return lax.all_to_all(copies, axes, split_axis=0, concat_axis=0, tiled=True)


def places(metas, row, col):
    delta = jnp.arange(N_COL, dtype=jnp.int32)
    p_cols = metas[:, :, :, :KP]
    entries = p_cols.reshape(N_ROW, N_COL, NB * KP)
    match = (entries // N_COL == row).astype(jnp.int32)
    earlier = jnp.cumsum(match, axis=2) - match
    order = jnp.arange(NB * KP, dtype=jnp.int32)
    sources = [
        lax.dynamic_index_in_dim(metas, (col + h * KA) % N_COL, 1, False) for h in range(2)
    ]
    result = []
    for t in range(2):
        chosen = match * (earlier == t)
        entry = jnp.sum(chosen * order, axis=2)
        u = jnp.sum(chosen * (entries % N_COL), axis=2)
        block = entry // KP
        far = (delta - col) % N_COL
        k, half = far % KA, far // KA
        quotient = jnp.zeros_like(u)
        for h in range(2):
            cells = sources[h]
            identity = jnp.broadcast_to(jnp.arange(NB, dtype=jnp.int32)[None, :, None], (N_ROW, NB, 1))
            picks = jnp.concatenate([identity, cells[:, :, KP:]], axis=2)
            hit = (block[:, :, None, None] == jnp.arange(NB)[None, None, :, None]) & (
                k[None, :, None, None] == jnp.arange(KA)[None, None, None, :]
            )
            pick = jnp.sum(jnp.where(hit, picks[:, None], 0), axis=(2, 3))
            value = jnp.sum(
                jnp.where(pick[:, :, None] == jnp.arange(NB), cells[:, None, :, h] // N_COL, 0), axis=2
            )
            quotient = jnp.where(half[None, :] == h, value, quotient)
        result.append(u * N_ROW + quotient)
    return jnp.stack(result, axis=2).reshape(-1)


def shifted(value, axis, steps):
    count = lax.axis_size(axis)
    return lax.ppermute(value, axis, [(i, (i + steps) % count) for i in range(count)])


def exchanged(value, axes):
    return lax.all_to_all(value, axes, split_axis=0, concat_axis=0, tiled=True)


META = KP + KA - 1
RELAYED = 2


def product_tables(cells, x, y):
    groups = jnp.arange(GROUP, dtype=jnp.int32)
    columns = [x * N_Y + (y + groups) % N_Y]
    back = (y + groups) // N_Y
    e_x = jnp.stack([(x - back - k2) % N_X for k2 in range(PAIR)])
    columns.append((e_x * N_Y + y).reshape(-1))
    wanted = jnp.concatenate(columns)
    chosen = (wanted[:, None] == jnp.arange(N_COL, dtype=jnp.int32)[None, :]).astype(f32)
    found = jnp.dot(chosen, cells, precision=lax.Precision.HIGHEST)
    found = (found + 0.5).astype(jnp.int32).reshape(-1, NB, META)
    entry_row = (found[:GROUP, :, :KP] // N_COL).reshape(GROUP, NB * KP)
    order = jnp.arange(NB * KP, dtype=jnp.int32)
    slot = jnp.sum(
        (entry_row[:, None, :] == entry_row[:, :, None]) & (order[None, None, :] < order[None, :, None]),
        axis=2,
        dtype=jnp.int32,
    )
    picks = [jnp.arange(NB, dtype=jnp.int32)]
    for k in range(1, KA):
        picks.append(found[GROUP + k, :, KP + k - 1])
    picks = jnp.stack(picks).reshape(PAIR, GROUP, NB)
    offset = jnp.where(groups == 0, 0, (back[None, :] + jnp.arange(PAIR)[:, None]) * NB)
    picks = (picks + offset[:, :, None]).transpose(1, 0, 2).reshape(GROUP, PAIR * NB)
    return jnp.concatenate([entry_row, slot, e_x.T % 2, e_x.T // 2, picks], axis=1).reshape(-1)


def on_device(a_blocks, a_live, p_blocks, p_cols, ghost_list, policy, rates, rhs, guess):
    x = lax.axis_index("x")
    y = lax.axis_index("y")
    row = lax.axis_index(ROW)
    col = x * N_Y + y
    own_p = p_blocks.reshape(NB, BS * KP, CB)
    p_one = shifted(own_p, "x", 1)
    meta = jnp.concatenate([p_cols, ghost_list], axis=1).astype(f32).reshape(-1)
    cells = to_all(meta, COL, N_COL)
    spare = -(-N_COL * NB * META // NCOL)
    spare = -(-spare // 8) * 8
    padded = jnp.pad(cells.reshape(-1), (0, spare * NCOL - cells.size)).reshape(spare, NCOL)
    packed = to_all(jnp.concatenate([guess, padded]), ROW, N_ROW)
    around = packed[:, :CB].reshape(N_ROW * CB, NCOL)
    metas = packed[:, CB:].reshape(N_ROW, spare * NCOL)[:, : cells.size]
    metas = (metas + 0.5).astype(jnp.int32).reshape(N_ROW, N_COL, NB, META)

    p_back = shifted(own_p[RELAYED:], "x", -1)
    p_rear = shifted(p_back, "x", -1)
    p_far = shifted(p_one[:RELAYED], "x", 1)
    parts = None
    numbers = jnp.concatenate([a_live.reshape(-1), policy])
    rate_rows = rates.reshape(-1, 1, BS)
    lefts = {}
    for group in (1, 3, 2, 0):
        left, parts = left_products(group, numbers, a_blocks, rate_rows, own_p, parts)
        lefts[group] = shifted(left, "y", -group) if group else left
    table = product_tables(cells, x, y)
    where = places(metas, row, col).reshape(N_ROW, N_X, N_Y, 2)
    where = where // (N_Y * N_ROW) * N_ROW + where % N_ROW
    own_cell = x * N_ROW + row
    prior = None
    stacked = None
    for group in (0, 1, 3, 2):
        near, far = own_p, p_one
        if group:
            if stacked is None:
                stacked = jnp.concatenate([own_p, p_one, p_far, p_rear])
            near = far = stacked
        sent = products(group, table, lefts[group], near, far)
        got = exchanged(sent.reshape(N_ROW * N_X, 2, CB, CB), PLANE)
        y_u = (y + group) % N_Y
        spots = lax.dynamic_index_in_dim(where, y_u, 2, False).reshape(-1)
        spots = jnp.concatenate([spots, jnp.stack([y_u, own_cell])])
        coarse, part, floor = gather(group, spots, got.reshape(COUNT, CB, CB), around, prior)
        if group == 0:
            floor_diag = floor
        prior = [coarse, part]
    coarse = coarse.reshape(N_COL * CB * N_ROW, CB)
    current = guess
    for sweep in range(2):
        if sweep:
            part = apply(coarse, to_all(current, ROW, N_ROW).reshape(N_ROW * CB, NCOL))
        pieces = exchanged(part.reshape(N_COL, CB, NCOL), COL)
        applied = jnp.sum(pieces, axis=0)
        current = current + damping * (rhs - applied) / floor_diag
    return coarse.reshape(N_COL * CB, N_ROW, 1, CB), current


def solution(mesh):
    mesh = Mesh(mesh.devices.reshape(N_ROW // 2, 2, N_X, N_Y), ALL)

    return jax.shard_map(
        on_device,
        mesh=mesh,
        in_specs=(
            P(ALL, None, None, None),
            P(ALL, None),
            P(ALL, None, None, None),
            P(ALL, None),
            P(ALL, None),
            P(ALL),
            P(),
            P(ALL, None),
            P(ALL, None),
        ),
        out_specs=(P(ROW, None, COL, None), P(ALL, None)),
        check_vma=False,
    )
```

```python
import functools

import jax
import jax.numpy as jnp
from jax import lax
from jax.experimental import pallas as pl
from jax.experimental.pallas import tpu as pltpu
from jax.sharding import Mesh, PartitionSpec as P

BS = 256
CB = 128
KA = 8
KP = 2
N_ROW = 8
N_COL = 16
NB = 8
NCOL = 256
damping = 0.7
f32 = jnp.float32
bf16 = jnp.bfloat16
ROW = ("z", "core")
COL = ("x", "y")
ALL = ROW + COL
PLANE = ROW + ("x",)
N_X = N_Y = 4
GROUP = 4
PAIR = 2


def split(value):
    high = value.astype(bf16)
    return high, (value - high.astype(f32)).astype(bf16)


def dot3(lhs, rhs):
    left = jnp.concatenate([lhs[0], lhs[0], lhs[1]], axis=1)
    right = jnp.concatenate([rhs[0], rhs[1], rhs[0]], axis=0)
    return jnp.dot(left, right, preferred_element_type=f32)


STEP = 2


def left_kernel(group, flips, table, a_ref, rate_a, rate_b, *rest):
    if flips:
        p_ref, out_ref, high_ref, low_ref = rest
    else:
        high_ref, low_ref, out_ref = rest
    step = pl.program_id(0)
    for r, rate_ref in enumerate((rate_a, rate_b)):
        s = step * STEP + r
        if flips:
            for m in range(KP):
                high, low = split(p_ref[r, pl.ds(m, BS, KP), :].T)
                high_ref[r, m * CB : (m + 1) * CB] = high
                low_ref[r, m * CB : (m + 1) * CB] = low
        for k2 in range(PAIR):
            block = a_ref[r, k2, 0] * table[s * KA + group + GROUP * k2].astype(f32)
            if group == 0 and k2 == 0:
                across = lax.broadcasted_iota(jnp.int32, (BS, BS), 0)
                along = lax.broadcasted_iota(jnp.int32, (BS, BS), 1)
                block = block + jnp.where(across == along, rate_ref[0], 0.0)
            out_ref[k2, r] = dot3((high_ref[r], low_ref[r]), split(block))


def left_products(group, table, a_blocks, rates, own_p, parts):
    half = pl.BlockSpec((STEP, KP * CB, BS), lambda s, t: (s, 0, 0))
    halves = [jax.ShapeDtypeStruct((NB, KP * CB, BS), bf16)] * 2
    flips = parts is None
    rate = lambda r: pl.BlockSpec((1, 1, BS), lambda s, t: (t[NB * KA + s * STEP + r], 0, 0))
    results = pl.pallas_call(
        functools.partial(left_kernel, group, flips),
        grid_spec=pltpu.PrefetchScalarGridSpec(
            num_scalar_prefetch=1,
            grid=(NB // STEP,),
            in_specs=[
                pl.BlockSpec((STEP, PAIR, 1, BS, BS), lambda s, t: (s, 0, group, 0, 0)),
                rate(0),
                rate(1),
            ]
            + ([pl.BlockSpec((STEP, KP * BS, CB), lambda s, t: (s, 0, 0))] if flips else [half, half]),
            out_specs=[pl.BlockSpec((PAIR, STEP, KP * CB, BS), lambda s, t: (0, s, 0, 0))]
            + ([half, half] if flips else []),
        ),
        out_shape=[jax.ShapeDtypeStruct((PAIR, NB, KP * CB, BS), f32)] + (halves if flips else []),
        cost_estimate=pl.CostEstimate(
            flops=NB * PAIR * 3 * 2 * BS**3,
            bytes_accessed=4 * PAIR * NB * 3 * BS * BS,
            transcendentals=0,
        ),
    )(table, a_blocks.reshape(NB, PAIR, GROUP, BS, BS), rates, rates, *([own_p] if flips else parts))
    return results[0], (list(results[1:]) if flips else parts)


ROW_AT, SLOT_AT, PARITY_AT, HALF_AT, PICK_AT, TABLE = 0, 16, 32, 34, 36, 52


def product_kernel(base, table, t_ref, *rest):
    sources, (out_ref, held, sems) = rest[: PAIR * STEP], rest[PAIR * STEP :]
    step = pl.program_id(0)

    def copy(step, r, m):
        entry = (step * STEP + r) * KP + m
        return pltpu.make_async_copy(
            held.at[lax.rem(step, 2), r, m],
            out_ref.at[table[base + ROW_AT + entry], :, :, table[base + SLOT_AT + entry]],
            sems.at[lax.rem(step, 2), r, m],
        )

    def each(step, act):
        for r in range(STEP):
            for m in range(KP):
                act(copy(step, r, m))

    @pl.when(step >= 2)
    def _():
        each(step - 2, lambda c: c.wait())

    now = lax.rem(step, 2)
    for r in range(STEP):
        for k2 in range(PAIR):
            ref = sources[r * PAIR + k2]
            ghost = jnp.concatenate(
                [ref[0, pl.ds(0, BS, KP), :], ref[0, pl.ds(1, BS, KP), :]], axis=1
            )
            result = dot3(split(t_ref[k2, r]), split(ghost))
            half, parity = table[base + HALF_AT + k2], table[base + PARITY_AT + k2]
            for m in range(KP):
                held[now, r, m, half, parity] = result[m * CB : (m + 1) * CB, :CB]
                held[now, r, m, 1 - half, parity] = result[m * CB : (m + 1) * CB, CB:]
    each(step, lambda c: c.start())

    @pl.when(step == NB // STEP - 1)
    def _():
        each(NB // STEP - 2, lambda c: c.wait())
        each(NB // STEP - 1, lambda c: c.wait())


def products(group, table, left, near, far):
    base = group * TABLE
    source = lambda r, k2: pl.BlockSpec(
        (1, KP * BS, CB), lambda s, t: (t[base + PICK_AT + k2 * NB + s * STEP + r], 0, 0)
    )
    return pl.pallas_call(
        functools.partial(product_kernel, base),
        grid_spec=pltpu.PrefetchScalarGridSpec(
            num_scalar_prefetch=1,
            grid=(NB // STEP,),
            in_specs=[pl.BlockSpec((PAIR, STEP, KP * CB, BS), lambda s, t: (0, s, 0, 0))]
            + [source(r, k2) for r in range(STEP) for k2 in range(PAIR)],
            out_specs=pl.BlockSpec(memory_space=pl.ANY),
            scratch_shapes=[
                pltpu.VMEM((2, STEP, KP, 2, 2, CB, CB), f32),
                pltpu.SemaphoreType.DMA((2, STEP, KP)),
            ],
        ),
        out_shape=jax.ShapeDtypeStruct((N_ROW, 2, 2, 2, CB, CB), f32),
        cost_estimate=pl.CostEstimate(
            flops=NB * PAIR * 3 * 2 * BS**3,
            bytes_accessed=4 * PAIR * NB * 3 * BS * BS,
            transcendentals=0,
        ),
    )(table, left, *[near, far] * STEP)


STEPS = 4
COUNT = 2 * N_ROW * N_X
PER_STEP = COUNT // STEPS
CELLS = N_X * N_ROW


def gather_kernel(group, table, got_ref, x_ref, *rest):
    coarse_ref, *part_refs, floor_ref, total, x_high, x_low = rest[-(N_X + 5) :]
    step = pl.program_id(0)

    @pl.when(step == 0)
    def _():
        total[...] = jnp.zeros_like(total)
        high, low = split(x_ref[...])
        x_high[...] = high
        x_low[...] = low

    @pl.loop(0, PER_STEP, step=4)
    def _(first):
        for b in range(4):
            place = table[step * PER_STEP + first + b]
            total[place] += got_ref[first + b]

    @pl.when(step == STEPS - 1)
    def _():
        rows = []
        for d in range(N_X):
            u = lax.rem(table[COUNT + 2] + d, N_X)
            blocks = [total[u * N_ROW + q] for q in range(N_ROW)]
            for q in range(N_ROW):
                coarse_ref[u, 0, pl.ds(q, CB, N_ROW), :] = blocks[q]
            rows.append(jnp.concatenate(blocks, axis=1))
        result = dot3(split(jnp.concatenate(rows)), (x_high[...], x_low[...]))
        for d in range(N_X):
            part_refs[d][...] = result[d * CB : (d + 1) * CB]
        if group == 0:
            across = lax.broadcasted_iota(jnp.int32, (CB, CB), 0)
            along = lax.broadcasted_iota(jnp.int32, (CB, CB), 1)
            own = jnp.where(across == along, total[table[COUNT + 1]], 0.0)
            diag = jnp.maximum(jnp.abs(jnp.sum(own, axis=1, keepdims=True)), 1.0)
            floor_ref[...] = jnp.broadcast_to(diag, (CB, NCOL))


def gather(group, table, got, x, prior):
    whole = lambda shape: pl.BlockSpec(shape, lambda i, t: (0,) * len(shape))
    in_specs = [
        pl.BlockSpec((PER_STEP, CB, CB), lambda i, t: (i, 0, 0)),
        whole((N_ROW * CB, NCOL)),
    ]
    args = [got, x]
    alias = {}
    if prior is not None:
        in_specs.append(pl.BlockSpec(memory_space=pl.ANY))
        args.append(prior)
        alias = {3: 0}
    coarse, *parts, floor = pl.pallas_call(
        functools.partial(gather_kernel, group),
        grid_spec=pltpu.PrefetchScalarGridSpec(
            num_scalar_prefetch=1,
            grid=(STEPS,),
            in_specs=in_specs,
            out_specs=[pl.BlockSpec((N_X, 1, CB * N_ROW, CB), lambda i, t: (0, t[COUNT], 0, 0))]
            + [whole((CB, NCOL))] * (N_X + 1),
            scratch_shapes=[
                pltpu.VMEM((CELLS, CB, CB), f32),
                pltpu.VMEM((N_ROW * CB, NCOL), bf16),
                pltpu.VMEM((N_ROW * CB, NCOL), bf16),
            ],
        ),
        out_shape=[jax.ShapeDtypeStruct((N_X, N_Y, CB * N_ROW, CB), f32)]
        + [jax.ShapeDtypeStruct((CB, NCOL), f32)] * (N_X + 1),
        input_output_aliases=alias,
        cost_estimate=pl.CostEstimate(
            flops=3 * 2 * N_X * CB * N_ROW * CB * NCOL,
            bytes_accessed=4 * (COUNT + CELLS + 2 * CELLS) * CB * CB,
            transcendentals=0,
        ),
    )(table, *args)
    return coarse, parts, floor


TALL = 4 * CB


def apply_kernel(c_ref, x_ref, out_ref, x_high, x_low):
    @pl.when(pl.program_id(0) == 0)
    def _():
        high, low = split(x_ref[...])
        x_high[...] = high
        x_low[...] = low

    rows = jnp.concatenate([c_ref[pl.ds(q, TALL, N_ROW), :] for q in range(N_ROW)], axis=1)
    out_ref[...] = dot3(split(rows), (x_high[...], x_low[...]))


def apply(coarse, x):
    return pl.pallas_call(
        apply_kernel,
        grid=(N_COL * CB // TALL,),
        in_specs=[
            pl.BlockSpec((TALL * N_ROW, CB), lambda u: (u, 0)),
            pl.BlockSpec((N_ROW * CB, NCOL), lambda u: (0, 0)),
        ],
        out_specs=pl.BlockSpec((TALL, NCOL), lambda u: (u, 0)),
        out_shape=jax.ShapeDtypeStruct((N_COL * CB, NCOL), f32),
        scratch_shapes=[pltpu.VMEM((N_ROW * CB, NCOL), bf16)] * 2,
    )(coarse, x)


def to_all(value, axes, count):
    copies = jnp.broadcast_to(value[None], (count,) + value.shape)
    return lax.all_to_all(copies, axes, split_axis=0, concat_axis=0, tiled=True)


def places(metas, row, col):
    delta = jnp.arange(N_COL, dtype=jnp.int32)
    p_cols = metas[:, :, :, :KP]
    entries = p_cols.reshape(N_ROW, N_COL, NB * KP)
    match = (entries // N_COL == row).astype(jnp.int32)
    earlier = jnp.cumsum(match, axis=2) - match
    order = jnp.arange(NB * KP, dtype=jnp.int32)
    sources = [
        lax.dynamic_index_in_dim(metas, (col + h * KA) % N_COL, 1, False) for h in range(2)
    ]
    result = []
    for t in range(2):
        chosen = match * (earlier == t)
        entry = jnp.sum(chosen * order, axis=2)
        u = jnp.sum(chosen * (entries % N_COL), axis=2)
        block = entry // KP
        far = (delta - col) % N_COL
        k, half = far % KA, far // KA
        quotient = jnp.zeros_like(u)
        for h in range(2):
            cells = sources[h]
            identity = jnp.broadcast_to(jnp.arange(NB, dtype=jnp.int32)[None, :, None], (N_ROW, NB, 1))
            picks = jnp.concatenate([identity, cells[:, :, KP:]], axis=2)
            hit = (block[:, :, None, None] == jnp.arange(NB)[None, None, :, None]) & (
                k[None, :, None, None] == jnp.arange(KA)[None, None, None, :]
            )
            pick = jnp.sum(jnp.where(hit, picks[:, None], 0), axis=(2, 3))
            value = jnp.sum(
                jnp.where(pick[:, :, None] == jnp.arange(NB), cells[:, None, :, h] // N_COL, 0), axis=2
            )
            quotient = jnp.where(half[None, :] == h, value, quotient)
        result.append(u * N_ROW + quotient)
    return jnp.stack(result, axis=2).reshape(-1)


def shifted(value, axis, steps):
    count = lax.axis_size(axis)
    return lax.ppermute(value, axis, [(i, (i + steps) % count) for i in range(count)])


def shifted_plane(value, x_steps, y_steps):
    pairs = [
        (a * N_Y + b, (a + x_steps) % N_X * N_Y + (b + y_steps) % N_Y)
        for a in range(N_X)
        for b in range(N_Y)
    ]
    return lax.ppermute(value, COL, pairs)


def exchanged(value, axes):
    return lax.all_to_all(value, axes, split_axis=0, concat_axis=0, tiled=True)


META = KP + KA - 1
RELAYED = 4
LAST = 2


def product_tables(cells, x, y):
    groups = jnp.arange(GROUP, dtype=jnp.int32)
    columns = [x * N_Y + (y + groups) % N_Y]
    back = (y + groups) // N_Y
    e_x = jnp.stack([(x - back - k2) % N_X for k2 in range(PAIR)])
    columns.append((e_x * N_Y + y).reshape(-1))
    wanted = jnp.concatenate(columns)
    chosen = (wanted[:, None] == jnp.arange(N_COL, dtype=jnp.int32)[None, :]).astype(f32)
    found = jnp.dot(chosen, cells, precision=lax.Precision.HIGHEST)
    found = (found + 0.5).astype(jnp.int32).reshape(-1, NB, META)
    entry_row = (found[:GROUP, :, :KP] // N_COL).reshape(GROUP, NB * KP)
    order = jnp.arange(NB * KP, dtype=jnp.int32)
    slot = jnp.sum(
        (entry_row[:, None, :] == entry_row[:, :, None]) & (order[None, None, :] < order[None, :, None]),
        axis=2,
        dtype=jnp.int32,
    )
    picks = [jnp.arange(NB, dtype=jnp.int32)]
    for k in range(1, KA):
        picks.append(found[GROUP + k, :, KP + k - 1])
    picks = jnp.stack(picks).reshape(PAIR, GROUP, NB)
    offset = jnp.where(groups == 0, 0, (back[None, :] + jnp.arange(PAIR)[:, None]) * NB)
    picks = (picks + offset[:, :, None]).transpose(1, 0, 2).reshape(GROUP, PAIR * NB)
    return jnp.concatenate([entry_row, slot, e_x.T % 2, e_x.T // 2, picks], axis=1).reshape(-1)


def on_device(a_blocks, a_live, p_blocks, p_cols, ghost_list, policy, rates, rhs, guess):
    x = lax.axis_index("x")
    y = lax.axis_index("y")
    row = lax.axis_index(ROW)
    col = x * N_Y + y
    own_p = p_blocks.reshape(NB, BS * KP, CB)
    p_one = shifted(own_p, "x", 1)
    meta = jnp.concatenate([p_cols, ghost_list], axis=1).astype(f32).reshape(-1)
    cells = to_all(meta, COL, N_COL)
    spare = -(-N_COL * NB * META // NCOL)
    spare = -(-spare // 8) * 8
    padded = jnp.pad(cells.reshape(-1), (0, spare * NCOL - cells.size)).reshape(spare, NCOL)
    packed = to_all(jnp.concatenate([guess, padded]), ROW, N_ROW)
    around = packed[:, :CB].reshape(N_ROW * CB, NCOL)
    metas = packed[:, CB:].reshape(N_ROW, spare * NCOL)[:, : cells.size]
    metas = (metas + 0.5).astype(jnp.int32).reshape(N_ROW, N_COL, NB, META)

    p_back = shifted(own_p[RELAYED:], "x", -1)
    p_rear = shifted(p_back, "x", -1)
    p_far = shifted(p_one[:RELAYED], "x", 1)
    parts = None
    numbers = jnp.concatenate([a_live.reshape(-1), policy])
    rate_rows = rates.reshape(-1, 1, BS)
    lefts = {}
    for group in (1, 3, 2, 0):
        left, parts = left_products(group, numbers, a_blocks, rate_rows, own_p, parts)
        lefts[group] = shifted(left, "y", -group) if group else left
    table = product_tables(cells, x, y)
    where = places(metas, row, col).reshape(N_ROW, N_X, N_Y, 2)
    where = where // (N_Y * N_ROW) * N_ROW + where % N_ROW
    own_cell = x * N_ROW + row
    coarse = None
    stacked = None
    sums = []
    for group in (0, 1, 3, LAST):
        near, far = own_p, p_one
        if group:
            if stacked is None:
                stacked = jnp.concatenate([own_p, p_one, p_far, p_rear])
            near = far = stacked
        sent = products(group, table, lefts[group], near, far)
        got = exchanged(sent.reshape(N_ROW * N_X, 2, CB, CB), PLANE)
        y_u = (y + group) % N_Y
        spots = lax.dynamic_index_in_dim(where, y_u, 2, False).reshape(-1)
        spots = jnp.concatenate([spots, jnp.stack([y_u, own_cell, x])])
        coarse, parts, floor = gather(group, spots, got.reshape(COUNT, CB, CB), around, coarse)
        if group == 0:
            floor_diag = floor
        if group != LAST:
            stack = jnp.stack(parts)
            sums.append(shifted(stack, "y", group) if group else stack)
    early = sums[0] + sums[1] + sums[2]
    applied = early[0]
    for d in range(1, N_X):
        applied = applied + shifted(early[d], "x", d)
    for d in range(N_X):
        applied = applied + shifted_plane(parts[d], d, LAST)
    current = guess + damping * (rhs - applied) / floor_diag

    coarse = coarse.reshape(N_COL * CB * N_ROW, CB)
    part = apply(coarse, to_all(current, ROW, N_ROW).reshape(N_ROW * CB, NCOL))
    applied = jnp.sum(exchanged(part.reshape(N_COL, CB, NCOL), COL), axis=0)
    current = current + damping * (rhs - applied) / floor_diag
    return coarse.reshape(N_COL * CB, N_ROW, 1, CB), current


def solution(mesh):
    mesh = Mesh(mesh.devices.reshape(N_ROW // 2, 2, N_X, N_Y), ALL)

    return jax.shard_map(
        on_device,
        mesh=mesh,
        in_specs=(
            P(ALL, None, None, None),
            P(ALL, None),
            P(ALL, None, None, None),
            P(ALL, None),
            P(ALL, None),
            P(ALL),
            P(),
            P(ALL, None),
            P(ALL, None),
        ),
        out_specs=(P(ROW, None, COL, None), P(ALL, None)),
        check_vma=False,
    )
```

```python
import functools

import jax
import jax.numpy as jnp
from jax import lax
from jax.experimental import pallas as pl
from jax.experimental.pallas import tpu as pltpu
from jax.sharding import Mesh, PartitionSpec as P

BS = 256
CB = 128
KA = 8
KP = 2
N_ROW = 8
N_COL = 16
NB = 8
NCOL = 256
damping = 0.7
f32 = jnp.float32
bf16 = jnp.bfloat16
ROW = ("z", "core")
COL = ("x", "y")
ALL = ROW + COL
PLANE = ROW + ("x",)
N_X = N_Y = 4
GROUP = 4
PAIR = 2


def split(value):
    high = value.astype(bf16)
    return high, (value - high.astype(f32)).astype(bf16)


def dot3(lhs, rhs):
    left = jnp.concatenate([lhs[0], lhs[0], lhs[1]], axis=1)
    right = jnp.concatenate([rhs[0], rhs[1], rhs[0]], axis=0)
    return jnp.dot(left, right, preferred_element_type=f32)


STEP = 2


def left_kernel(group, flips, table, a_ref, rate_a, rate_b, *rest):
    if flips:
        p_ref, out_ref, high_ref, low_ref = rest
    else:
        high_ref, low_ref, out_ref = rest
    step = pl.program_id(0)
    for r, rate_ref in enumerate((rate_a, rate_b)):
        s = step * STEP + r
        if flips:
            for m in range(KP):
                high, low = split(p_ref[r, pl.ds(m, BS, KP), :].T)
                high_ref[r, m * CB : (m + 1) * CB] = high
                low_ref[r, m * CB : (m + 1) * CB] = low
        for k2 in range(PAIR):
            block = a_ref[r, k2, 0] * table[s * KA + group + GROUP * k2].astype(f32)
            if group == 0 and k2 == 0:
                across = lax.broadcasted_iota(jnp.int32, (BS, BS), 0)
                along = lax.broadcasted_iota(jnp.int32, (BS, BS), 1)
                block = block + jnp.where(across == along, rate_ref[0], 0.0)
            out_ref[k2, r] = dot3((high_ref[r], low_ref[r]), split(block))


def left_products(group, table, a_blocks, rates, own_p, parts):
    half = pl.BlockSpec((STEP, KP * CB, BS), lambda s, t: (s, 0, 0))
    halves = [jax.ShapeDtypeStruct((NB, KP * CB, BS), bf16)] * 2
    flips = parts is None
    rate = lambda r: pl.BlockSpec((1, 1, BS), lambda s, t: (t[NB * KA + s * STEP + r], 0, 0))
    results = pl.pallas_call(
        functools.partial(left_kernel, group, flips),
        grid_spec=pltpu.PrefetchScalarGridSpec(
            num_scalar_prefetch=1,
            grid=(NB // STEP,),
            in_specs=[
                pl.BlockSpec((STEP, PAIR, 1, BS, BS), lambda s, t: (s, 0, group, 0, 0)),
                rate(0),
                rate(1),
            ]
            + ([pl.BlockSpec((STEP, KP * BS, CB), lambda s, t: (s, 0, 0))] if flips else [half, half]),
            out_specs=[pl.BlockSpec((PAIR, STEP, KP * CB, BS), lambda s, t: (0, s, 0, 0))]
            + ([half, half] if flips else []),
        ),
        out_shape=[jax.ShapeDtypeStruct((PAIR, NB, KP * CB, BS), f32)] + (halves if flips else []),
        cost_estimate=pl.CostEstimate(
            flops=NB * PAIR * 3 * 2 * BS**3,
            bytes_accessed=4 * PAIR * NB * 3 * BS * BS,
            transcendentals=0,
        ),
    )(table, a_blocks.reshape(NB, PAIR, GROUP, BS, BS), rates, rates, *([own_p] if flips else parts))
    return results[0], (list(results[1:]) if flips else parts)


ROW_AT, SLOT_AT, PARITY_AT, HALF_AT, PICK_AT, TABLE = 0, 16, 32, 34, 36, 52


def product_kernel(base, lane, table, t_ref, *rest):
    sources, (out_ref, held, sems) = rest[: PAIR * STEP], rest[-3:]
    step = pl.program_id(0)

    def copy(step, r, m):
        entry = (step * STEP + r) * KP + m
        return pltpu.make_async_copy(
            held.at[lax.rem(step, 2), r, m],
            out_ref.at[table[base + ROW_AT + entry], :, :, lane, table[base + SLOT_AT + entry]],
            sems.at[lax.rem(step, 2), r, m],
        )

    def each(step, act):
        for r in range(STEP):
            for m in range(KP):
                act(copy(step, r, m))

    @pl.when(step >= 2)
    def _():
        each(step - 2, lambda c: c.wait())

    now = lax.rem(step, 2)
    for r in range(STEP):
        for k2 in range(PAIR):
            ref = sources[r * PAIR + k2]
            ghost = jnp.concatenate(
                [ref[0, pl.ds(0, BS, KP), :], ref[0, pl.ds(1, BS, KP), :]], axis=1
            )
            result = dot3(split(t_ref[k2, r]), split(ghost))
            half, parity = table[base + HALF_AT + k2], table[base + PARITY_AT + k2]
            for m in range(KP):
                held[now, r, m, half, parity] = result[m * CB : (m + 1) * CB, :CB]
                held[now, r, m, 1 - half, parity] = result[m * CB : (m + 1) * CB, CB:]
    each(step, lambda c: c.start())

    @pl.when(step == NB // STEP - 1)
    def _():
        each(NB // STEP - 2, lambda c: c.wait())
        each(NB // STEP - 1, lambda c: c.wait())


def products(group, lane, lanes, table, left, near, far, prior):
    before = [] if prior is None else [prior]
    base = group * TABLE
    source = lambda r, k2: pl.BlockSpec(
        (1, KP * BS, CB), lambda s, t: (t[base + PICK_AT + k2 * NB + s * STEP + r], 0, 0)
    )
    return pl.pallas_call(
        functools.partial(product_kernel, base, lane),
        grid_spec=pltpu.PrefetchScalarGridSpec(
            num_scalar_prefetch=1,
            grid=(NB // STEP,),
            in_specs=[pl.BlockSpec((PAIR, STEP, KP * CB, BS), lambda s, t: (0, s, 0, 0))]
            + [source(r, k2) for r in range(STEP) for k2 in range(PAIR)]
            + [pl.BlockSpec(memory_space=pl.ANY)] * len(before),
            out_specs=pl.BlockSpec(memory_space=pl.ANY),
            scratch_shapes=[
                pltpu.VMEM((2, STEP, KP, 2, 2, CB, CB), f32),
                pltpu.SemaphoreType.DMA((2, STEP, KP)),
            ],
        ),
        out_shape=jax.ShapeDtypeStruct((N_ROW, 2, 2, lanes, 2, CB, CB), f32),
        input_output_aliases={2 + PAIR * STEP: 0} if before else {},
        cost_estimate=pl.CostEstimate(
            flops=NB * PAIR * 3 * 2 * BS**3,
            bytes_accessed=4 * PAIR * NB * 3 * BS * BS,
            transcendentals=0,
        ),
    )(table, left, *[near, far] * STEP, *before)


STEPS = 4
COUNT = 2 * N_ROW * N_X
PER_STEP = COUNT // STEPS
CELLS = N_X * N_ROW


def gather_kernel(group, table, got_ref, x_ref, *rest):
    coarse_ref, *part_refs, floor_ref, total, x_high, x_low = rest[-(N_X + 5) :]
    step = pl.program_id(0)

    @pl.when(step == 0)
    def _():
        total[...] = jnp.zeros_like(total)
        high, low = split(x_ref[...])
        x_high[...] = high
        x_low[...] = low

    @pl.loop(0, PER_STEP, step=4)
    def _(first):
        for b in range(4):
            place = table[step * PER_STEP + first + b]
            total[place] += got_ref[first // 2 + b // 2, 0, b % 2]

    @pl.when(step == STEPS - 1)
    def _():
        rows = []
        for d in range(N_X):
            u = lax.rem(table[COUNT + 2] + d, N_X)
            blocks = [total[u * N_ROW + q] for q in range(N_ROW)]
            for q in range(N_ROW):
                coarse_ref[u, 0, pl.ds(q, CB, N_ROW), :] = blocks[q]
            rows.append(jnp.concatenate(blocks, axis=1))
        result = dot3(split(jnp.concatenate(rows)), (x_high[...], x_low[...]))
        for d in range(N_X):
            part_refs[d][...] = result[d * CB : (d + 1) * CB]
        if group == 0:
            across = lax.broadcasted_iota(jnp.int32, (CB, CB), 0)
            along = lax.broadcasted_iota(jnp.int32, (CB, CB), 1)
            own = jnp.where(across == along, total[table[COUNT + 1]], 0.0)
            diag = jnp.maximum(jnp.abs(jnp.sum(own, axis=1, keepdims=True)), 1.0)
            floor_ref[...] = jnp.broadcast_to(diag, (CB, NCOL))


def gather(group, lane, table, got, x, prior):
    whole = lambda shape: pl.BlockSpec(shape, lambda i, t: (0,) * len(shape))
    in_specs = [
        pl.BlockSpec((PER_STEP // 2, 1, 2, CB, CB), lambda i, t: (i, lane, 0, 0, 0)),
        whole((N_ROW * CB, NCOL)),
    ]
    args = [got, x]
    alias = {}
    if prior is not None:
        in_specs.append(pl.BlockSpec(memory_space=pl.ANY))
        args.append(prior)
        alias = {3: 0}
    coarse, *parts, floor = pl.pallas_call(
        functools.partial(gather_kernel, group),
        grid_spec=pltpu.PrefetchScalarGridSpec(
            num_scalar_prefetch=1,
            grid=(STEPS,),
            in_specs=in_specs,
            out_specs=[pl.BlockSpec((N_X, 1, CB * N_ROW, CB), lambda i, t: (0, t[COUNT], 0, 0))]
            + [whole((CB, NCOL))] * (N_X + 1),
            scratch_shapes=[
                pltpu.VMEM((CELLS, CB, CB), f32),
                pltpu.VMEM((N_ROW * CB, NCOL), bf16),
                pltpu.VMEM((N_ROW * CB, NCOL), bf16),
            ],
        ),
        out_shape=[jax.ShapeDtypeStruct((N_X, N_Y, CB * N_ROW, CB), f32)]
        + [jax.ShapeDtypeStruct((CB, NCOL), f32)] * (N_X + 1),
        input_output_aliases=alias,
        cost_estimate=pl.CostEstimate(
            flops=3 * 2 * N_X * CB * N_ROW * CB * NCOL,
            bytes_accessed=4 * (COUNT + CELLS + 2 * CELLS) * CB * CB,
            transcendentals=0,
        ),
    )(table, *args)
    return coarse, parts, floor


TALL = 4 * CB


def apply_kernel(c_ref, x_ref, out_ref, x_high, x_low):
    @pl.when(pl.program_id(0) == 0)
    def _():
        high, low = split(x_ref[...])
        x_high[...] = high
        x_low[...] = low

    rows = jnp.concatenate([c_ref[pl.ds(q, TALL, N_ROW), :] for q in range(N_ROW)], axis=1)
    out_ref[...] = dot3(split(rows), (x_high[...], x_low[...]))


def apply(coarse, x):
    return pl.pallas_call(
        apply_kernel,
        grid=(N_COL * CB // TALL,),
        in_specs=[
            pl.BlockSpec((TALL * N_ROW, CB), lambda u: (u, 0)),
            pl.BlockSpec((N_ROW * CB, NCOL), lambda u: (0, 0)),
        ],
        out_specs=pl.BlockSpec((TALL, NCOL), lambda u: (u, 0)),
        out_shape=jax.ShapeDtypeStruct((N_COL * CB, NCOL), f32),
        scratch_shapes=[pltpu.VMEM((N_ROW * CB, NCOL), bf16)] * 2,
    )(coarse, x)


def to_all(value, axes, count):
    copies = jnp.broadcast_to(value[None], (count,) + value.shape)
    return lax.all_to_all(copies, axes, split_axis=0, concat_axis=0, tiled=True)


def places(metas, row, col):
    delta = jnp.arange(N_COL, dtype=jnp.int32)
    p_cols = metas[:, :, :, :KP]
    entries = p_cols.reshape(N_ROW, N_COL, NB * KP)
    match = (entries // N_COL == row).astype(jnp.int32)
    earlier = jnp.cumsum(match, axis=2) - match
    order = jnp.arange(NB * KP, dtype=jnp.int32)
    sources = [
        lax.dynamic_index_in_dim(metas, (col + h * KA) % N_COL, 1, False) for h in range(2)
    ]
    result = []
    for t in range(2):
        chosen = match * (earlier == t)
        entry = jnp.sum(chosen * order, axis=2)
        u = jnp.sum(chosen * (entries % N_COL), axis=2)
        block = entry // KP
        far = (delta - col) % N_COL
        k, half = far % KA, far // KA
        quotient = jnp.zeros_like(u)
        for h in range(2):
            cells = sources[h]
            identity = jnp.broadcast_to(jnp.arange(NB, dtype=jnp.int32)[None, :, None], (N_ROW, NB, 1))
            picks = jnp.concatenate([identity, cells[:, :, KP:]], axis=2)
            hit = (block[:, :, None, None] == jnp.arange(NB)[None, None, :, None]) & (
                k[None, :, None, None] == jnp.arange(KA)[None, None, None, :]
            )
            pick = jnp.sum(jnp.where(hit, picks[:, None], 0), axis=(2, 3))
            value = jnp.sum(
                jnp.where(pick[:, :, None] == jnp.arange(NB), cells[:, None, :, h] // N_COL, 0), axis=2
            )
            quotient = jnp.where(half[None, :] == h, value, quotient)
        result.append(u * N_ROW + quotient)
    return jnp.stack(result, axis=2).reshape(-1)


def shifted(value, axis, steps):
    count = lax.axis_size(axis)
    return lax.ppermute(value, axis, [(i, (i + steps) % count) for i in range(count)])


def shifted_plane(value, x_steps, y_steps):
    pairs = [
        (a * N_Y + b, (a + x_steps) % N_X * N_Y + (b + y_steps) % N_Y)
        for a in range(N_X)
        for b in range(N_Y)
    ]
    return lax.ppermute(value, COL, pairs)


def exchanged(value, axes):
    return lax.all_to_all(value, axes, split_axis=0, concat_axis=0, tiled=True)


META = KP + KA - 1
RELAYED = 4
LAST = 2


def product_tables(cells, x, y):
    groups = jnp.arange(GROUP, dtype=jnp.int32)
    columns = [x * N_Y + (y + groups) % N_Y]
    back = (y + groups) // N_Y
    e_x = jnp.stack([(x - back - k2) % N_X for k2 in range(PAIR)])
    columns.append((e_x * N_Y + y).reshape(-1))
    wanted = jnp.concatenate(columns)
    chosen = (wanted[:, None] == jnp.arange(N_COL, dtype=jnp.int32)[None, :]).astype(f32)
    found = jnp.dot(chosen, cells, precision=lax.Precision.HIGHEST)
    found = (found + 0.5).astype(jnp.int32).reshape(-1, NB, META)
    entry_row = (found[:GROUP, :, :KP] // N_COL).reshape(GROUP, NB * KP)
    order = jnp.arange(NB * KP, dtype=jnp.int32)
    slot = jnp.sum(
        (entry_row[:, None, :] == entry_row[:, :, None]) & (order[None, None, :] < order[None, :, None]),
        axis=2,
        dtype=jnp.int32,
    )
    picks = [jnp.arange(NB, dtype=jnp.int32)]
    for k in range(1, KA):
        picks.append(found[GROUP + k, :, KP + k - 1])
    picks = jnp.stack(picks).reshape(PAIR, GROUP, NB)
    offset = jnp.where(groups == 0, 0, (back[None, :] + jnp.arange(PAIR)[:, None]) * NB)
    picks = (picks + offset[:, :, None]).transpose(1, 0, 2).reshape(GROUP, PAIR * NB)
    return jnp.concatenate([entry_row, slot, e_x.T % 2, e_x.T // 2, picks], axis=1).reshape(-1)


def on_device(a_blocks, a_live, p_blocks, p_cols, ghost_list, policy, rates, rhs, guess):
    x = lax.axis_index("x")
    y = lax.axis_index("y")
    row = lax.axis_index(ROW)
    col = x * N_Y + y
    own_p = p_blocks.reshape(NB, BS * KP, CB)
    p_one = shifted(own_p, "x", 1)
    meta = jnp.concatenate([p_cols, ghost_list], axis=1).astype(f32).reshape(-1)
    cells = to_all(meta, COL, N_COL)
    spare = -(-N_COL * NB * META // NCOL)
    spare = -(-spare // 8) * 8
    padded = jnp.pad(cells.reshape(-1), (0, spare * NCOL - cells.size)).reshape(spare, NCOL)
    packed = to_all(jnp.concatenate([guess, padded]), ROW, N_ROW)
    around = packed[:, :CB].reshape(N_ROW * CB, NCOL)
    metas = packed[:, CB:].reshape(N_ROW, spare * NCOL)[:, : cells.size]
    metas = (metas + 0.5).astype(jnp.int32).reshape(N_ROW, N_COL, NB, META)

    p_back = shifted(own_p[RELAYED:], "x", -1)
    p_rear = shifted(p_back, "x", -1)
    p_far = shifted(p_one[:RELAYED], "x", 1)
    parts = None
    numbers = jnp.concatenate([a_live.reshape(-1), policy])
    rate_rows = rates.reshape(-1, 1, BS)
    lefts = {}
    for group in (1, 3, 2, 0):
        left, parts = left_products(group, numbers, a_blocks, rate_rows, own_p, parts)
        lefts[group] = shifted(left, "y", -group) if group else left
    table = product_tables(cells, x, y)
    where = places(metas, row, col).reshape(N_ROW, N_X, N_Y, 2)
    where = where // (N_Y * N_ROW) * N_ROW + where % N_ROW
    own_cell = x * N_ROW + row
    coarse = None
    stacked = None
    sums = []
    for batch in ((0,), (1, 3), (LAST,)):
        sent = None
        for lane, group in enumerate(batch):
            near, far = own_p, p_one
            if group:
                if stacked is None:
                    stacked = jnp.concatenate([own_p, p_one, p_far, p_rear])
                near = far = stacked
            sent = products(group, lane, len(batch), table, lefts[group], near, far, sent)
        got = exchanged(sent.reshape(N_ROW * N_X, len(batch), 2, CB, CB), PLANE)
        for lane, group in enumerate(batch):
            y_u = (y + group) % N_Y
            spots = lax.dynamic_index_in_dim(where, y_u, 2, False).reshape(-1)
            spots = jnp.concatenate([spots, jnp.stack([y_u, own_cell, x])])
            coarse, parts, floor = gather(group, lane, spots, got, around, coarse)
            if group == 0:
                floor_diag = floor
            if group != LAST:
                stack = jnp.stack(parts)
                sums.append(shifted(stack, "y", group) if group else stack)
    early = sums[0] + sums[1] + sums[2]
    applied = early[0]
    for d in range(1, N_X):
        applied = applied + shifted(early[d], "x", d)
    for d in range(N_X):
        applied = applied + shifted_plane(parts[d], d, LAST)
    current = guess + damping * (rhs - applied) / floor_diag

    coarse = coarse.reshape(N_COL * CB * N_ROW, CB)
    part = apply(coarse, to_all(current, ROW, N_ROW).reshape(N_ROW * CB, NCOL))
    applied = jnp.sum(exchanged(part.reshape(N_COL, CB, NCOL), COL), axis=0)
    current = current + damping * (rhs - applied) / floor_diag
    return coarse.reshape(N_COL * CB, N_ROW, 1, CB), current


def solution(mesh):
    mesh = Mesh(mesh.devices.reshape(N_ROW // 2, 2, N_X, N_Y), ALL)

    return jax.shard_map(
        on_device,
        mesh=mesh,
        in_specs=(
            P(ALL, None, None, None),
            P(ALL, None),
            P(ALL, None, None, None),
            P(ALL, None),
            P(ALL, None),
            P(ALL),
            P(),
            P(ALL, None),
            P(ALL, None),
        ),
        out_specs=(P(ROW, None, COL, None), P(ALL, None)),
        check_vma=False,
    )
```

```python
import functools

import jax
import jax.numpy as jnp
from jax import lax
from jax.experimental import pallas as pl
from jax.experimental.pallas import tpu as pltpu
from jax.sharding import Mesh, PartitionSpec as P

BS = 256
CB = 128
KA = 8
KP = 2
N_ROW = 8
N_COL = 16
NB = 8
NCOL = 256
damping = 0.7
f32 = jnp.float32
bf16 = jnp.bfloat16
ROW = ("z", "core")
COL = ("x", "y")
ALL = ROW + COL
PLANE = ROW + ("x",)
N_X = N_Y = 4
GROUP = 4
PAIR = 2


def split(value):
    high = value.astype(bf16)
    return high, (value - high.astype(f32)).astype(bf16)


def dot3(lhs, rhs):
    left = jnp.concatenate([lhs[0], lhs[0], lhs[1]], axis=1)
    right = jnp.concatenate([rhs[0], rhs[1], rhs[0]], axis=0)
    return jnp.dot(left, right, preferred_element_type=f32)


STEP = 2


def left_kernel(group, flips, live, policy, a_ref, *rest):
    rates = ()
    if group == 0:
        rates, rest = rest[:STEP], rest[STEP:]
    if flips:
        p_ref, out_ref, high_ref, low_ref = rest
    else:
        high_ref, low_ref, out_ref = rest
    step = pl.program_id(0)
    for r in range(STEP):
        s = step * STEP + r
        if flips:
            for m in range(KP):
                high, low = split(p_ref[r, pl.ds(m, BS, KP), :].T)
                high_ref[r, m * CB : (m + 1) * CB] = high
                low_ref[r, m * CB : (m + 1) * CB] = low
        for k2 in range(PAIR):
            block = a_ref[r, k2, 0] * live[s, group + GROUP * k2].astype(f32)
            if group == 0 and k2 == 0:
                across = lax.broadcasted_iota(jnp.int32, (BS, BS), 0)
                along = lax.broadcasted_iota(jnp.int32, (BS, BS), 1)
                block = block + jnp.where(across == along, rates[r][0], 0.0)
            out_ref[k2, r] = dot3((high_ref[r], low_ref[r]), split(block))


def left_products(group, live, policy, a_blocks, rates, own_p, parts):
    half = pl.BlockSpec((STEP, KP * CB, BS), lambda s, t, p: (s, 0, 0))
    halves = [jax.ShapeDtypeStruct((NB, KP * CB, BS), bf16)] * 2
    flips = parts is None
    rate = lambda r: pl.BlockSpec((1, 1, BS), lambda s, t, p: (p[s * STEP + r], 0, 0))
    results = pl.pallas_call(
        functools.partial(left_kernel, group, flips),
        grid_spec=pltpu.PrefetchScalarGridSpec(
            num_scalar_prefetch=2,
            grid=(NB // STEP,),
            in_specs=[pl.BlockSpec((STEP, PAIR, 1, BS, BS), lambda s, t, p: (s, 0, group, 0, 0))]
            + ([rate(r) for r in range(STEP)] if group == 0 else [])
            + ([pl.BlockSpec((STEP, KP * BS, CB), lambda s, t, p: (s, 0, 0))] if flips else [half, half]),
            out_specs=[pl.BlockSpec((PAIR, STEP, KP * CB, BS), lambda s, t, p: (0, s, 0, 0))]
            + ([half, half] if flips else []),
        ),
        out_shape=[jax.ShapeDtypeStruct((PAIR, NB, KP * CB, BS), f32)] + (halves if flips else []),
        cost_estimate=pl.CostEstimate(
            flops=NB * PAIR * 3 * 2 * BS**3,
            bytes_accessed=4 * PAIR * NB * 3 * BS * BS,
            transcendentals=0,
        ),
    )(
        live,
        policy,
        a_blocks.reshape(NB, PAIR, GROUP, BS, BS),
        *([rates] * STEP if group == 0 else []),
        *([own_p] if flips else parts),
    )
    return results[0], (list(results[1:]) if flips else parts)


ROW_AT, SLOT_AT, PARITY_AT, HALF_AT, PICK_AT, TABLE = 0, 16, 32, 34, 36, 52


def product_kernel(base, lane, table, t_ref, *rest):
    sources, (out_ref, held, sems) = rest[: PAIR * STEP], rest[-3:]
    step = pl.program_id(0)

    def copy(step, r, m):
        entry = (step * STEP + r) * KP + m
        return pltpu.make_async_copy(
            held.at[lax.rem(step, 2), r, m],
            out_ref.at[table[base + ROW_AT + entry], :, :, lane, table[base + SLOT_AT + entry]],
            sems.at[lax.rem(step, 2), r, m],
        )

    def each(step, act):
        for r in range(STEP):
            for m in range(KP):
                act(copy(step, r, m))

    @pl.when(step >= 2)
    def _():
        each(step - 2, lambda c: c.wait())

    now = lax.rem(step, 2)
    for r in range(STEP):
        for k2 in range(PAIR):
            ref = sources[r * PAIR + k2]
            ghost = jnp.concatenate(
                [ref[0, pl.ds(0, BS, KP), :], ref[0, pl.ds(1, BS, KP), :]], axis=1
            )
            result = dot3(split(t_ref[k2, r]), split(ghost))
            half, parity = table[base + HALF_AT + k2], table[base + PARITY_AT + k2]
            for m in range(KP):
                held[now, r, m, half, parity] = result[m * CB : (m + 1) * CB, :CB]
                held[now, r, m, 1 - half, parity] = result[m * CB : (m + 1) * CB, CB:]
    each(step, lambda c: c.start())

    @pl.when(step == NB // STEP - 1)
    def _():
        each(NB // STEP - 2, lambda c: c.wait())
        each(NB // STEP - 1, lambda c: c.wait())


def products(group, lane, lanes, table, left, near, far, prior):
    before = [] if prior is None else [prior]
    base = group * TABLE
    source = lambda r, k2: pl.BlockSpec(
        (1, KP * BS, CB), lambda s, t: (t[base + PICK_AT + k2 * NB + s * STEP + r], 0, 0)
    )
    return pl.pallas_call(
        functools.partial(product_kernel, base, lane),
        grid_spec=pltpu.PrefetchScalarGridSpec(
            num_scalar_prefetch=1,
            grid=(NB // STEP,),
            in_specs=[pl.BlockSpec((PAIR, STEP, KP * CB, BS), lambda s, t: (0, s, 0, 0))]
            + [source(r, k2) for r in range(STEP) for k2 in range(PAIR)]
            + [pl.BlockSpec(memory_space=pl.ANY)] * len(before),
            out_specs=pl.BlockSpec(memory_space=pl.ANY),
            scratch_shapes=[
                pltpu.VMEM((2, STEP, KP, 2, 2, CB, CB), f32),
                pltpu.SemaphoreType.DMA((2, STEP, KP)),
            ],
        ),
        out_shape=jax.ShapeDtypeStruct((N_ROW, 2, 2, lanes, 2, CB, CB), f32),
        input_output_aliases={2 + PAIR * STEP: 0} if before else {},
        cost_estimate=pl.CostEstimate(
            flops=NB * PAIR * 3 * 2 * BS**3,
            bytes_accessed=4 * PAIR * NB * 3 * BS * BS,
            transcendentals=0,
        ),
    )(table, left, *[near, far] * STEP, *before)


STEPS = 4
COUNT = 2 * N_ROW * N_X
PER_STEP = COUNT // STEPS
CELLS = N_X * N_ROW


def gather_kernel(group, table, got_ref, x_ref, *rest):
    coarse_ref, high_ref, low_ref, *part_refs, floor_ref, total, x_high, x_low = rest[-(N_X + 7) :]
    step = pl.program_id(0)

    @pl.when(step == 0)
    def _():
        total[...] = jnp.zeros_like(total)
        high, low = split(x_ref[...])
        x_high[...] = high
        x_low[...] = low

    @pl.loop(0, PER_STEP, step=4)
    def _(first):
        for b in range(4):
            place = table[step * PER_STEP + first + b]
            total[place] += got_ref[first // 2 + b // 2, 0, b % 2]

    @pl.when(step == STEPS - 1)
    def _():
        rows = []
        for d in range(N_X):
            u = lax.rem(table[COUNT + 2] + d, N_X)
            blocks = [total[u * N_ROW + q] for q in range(N_ROW)]
            for q in range(N_ROW):
                coarse_ref[u, 0, pl.ds(q, CB, N_ROW), :] = blocks[q]
            rows.append(jnp.concatenate(blocks, axis=1))
        high, low = split(jnp.concatenate(rows))
        result = dot3((high, low), (x_high[...], x_low[...]))
        for d in range(N_X):
            u = lax.rem(table[COUNT + 2] + d, N_X)
            mine = slice(d * CB, (d + 1) * CB)
            high_ref[u, 0] = high[mine]
            low_ref[u, 0] = low[mine]
            part_refs[d][...] = result[mine]
        if group == 0:
            across = lax.broadcasted_iota(jnp.int32, (CB, CB), 0)
            along = lax.broadcasted_iota(jnp.int32, (CB, CB), 1)
            own = jnp.where(across == along, total[table[COUNT + 1]], 0.0)
            diag = jnp.maximum(jnp.abs(jnp.sum(own, axis=1, keepdims=True)), 1.0)
            floor_ref[...] = jnp.broadcast_to(diag, (CB, NCOL))


def gather(group, lane, table, got, x, prior):
    whole = lambda shape: pl.BlockSpec(shape, lambda i, t: (0,) * len(shape))
    in_specs = [
        pl.BlockSpec((PER_STEP // 2, 1, 2, CB, CB), lambda i, t: (i, lane, 0, 0, 0)),
        whole((N_ROW * CB, NCOL)),
    ]
    args = [got, x]
    alias = {}
    if prior is not None:
        in_specs += [pl.BlockSpec(memory_space=pl.ANY)] * len(prior)
        args += prior
        alias = {3: 0, 4: 1, 5: 2}
    rows = pl.BlockSpec((N_X, 1, CB, N_ROW * CB), lambda i, t: (0, t[COUNT], 0, 0))
    *made, floor = pl.pallas_call(
        functools.partial(gather_kernel, group),
        grid_spec=pltpu.PrefetchScalarGridSpec(
            num_scalar_prefetch=1,
            grid=(STEPS,),
            in_specs=in_specs,
            out_specs=[pl.BlockSpec((N_X, 1, CB * N_ROW, CB), lambda i, t: (0, t[COUNT], 0, 0)), rows, rows]
            + [whole((CB, NCOL))] * (N_X + 1),
            scratch_shapes=[
                pltpu.VMEM((CELLS, CB, CB), f32),
                pltpu.VMEM((N_ROW * CB, NCOL), bf16),
                pltpu.VMEM((N_ROW * CB, NCOL), bf16),
            ],
        ),
        out_shape=[jax.ShapeDtypeStruct((N_X, N_Y, CB * N_ROW, CB), f32)]
        + [jax.ShapeDtypeStruct((N_X, N_Y, CB, N_ROW * CB), bf16)] * 2
        + [jax.ShapeDtypeStruct((CB, NCOL), f32)] * (N_X + 1),
        input_output_aliases=alias,
        cost_estimate=pl.CostEstimate(
            flops=3 * 2 * N_X * CB * N_ROW * CB * NCOL,
            bytes_accessed=4 * (COUNT + CELLS + 2 * CELLS) * CB * CB,
            transcendentals=0,
        ),
    )(table, *args)
    return made[:3], made[3:], floor


TALL = 4 * CB


def apply_kernel(high_ref, low_ref, x_ref, out_ref, x_high, x_low):
    @pl.when(pl.program_id(0) == 0)
    def _():
        high, low = split(x_ref[...])
        x_high[...] = high
        x_low[...] = low

    out_ref[...] = dot3((high_ref[...], low_ref[...]), (x_high[...], x_low[...]))


def apply(high, low, x):
    rows = pl.BlockSpec((TALL, N_ROW * CB), lambda u: (u, 0))
    return pl.pallas_call(
        apply_kernel,
        grid=(N_COL * CB // TALL,),
        in_specs=[rows, rows, pl.BlockSpec((N_ROW * CB, NCOL), lambda u: (0, 0))],
        out_specs=pl.BlockSpec((TALL, NCOL), lambda u: (u, 0)),
        out_shape=jax.ShapeDtypeStruct((N_COL * CB, NCOL), f32),
        scratch_shapes=[pltpu.VMEM((N_ROW * CB, NCOL), bf16)] * 2,
    )(high, low, x)


def to_all(value, axes, count):
    copies = jnp.broadcast_to(value[None], (count,) + value.shape)
    return lax.all_to_all(copies, axes, split_axis=0, concat_axis=0, tiled=True)


def places(metas, row, col):
    delta = jnp.arange(N_COL, dtype=jnp.int32)
    p_cols = metas[:, :, :, :KP]
    entries = p_cols.reshape(N_ROW, N_COL, NB * KP)
    match = (entries // N_COL == row).astype(jnp.int32)
    earlier = jnp.cumsum(match, axis=2) - match
    order = jnp.arange(NB * KP, dtype=jnp.int32)
    sources = [
        lax.dynamic_index_in_dim(metas, (col + h * KA) % N_COL, 1, False) for h in range(2)
    ]
    result = []
    for t in range(2):
        chosen = match * (earlier == t)
        entry = jnp.sum(chosen * order, axis=2)
        u = jnp.sum(chosen * (entries % N_COL), axis=2)
        block = entry // KP
        far = (delta - col) % N_COL
        k, half = far % KA, far // KA
        quotient = jnp.zeros_like(u)
        for h in range(2):
            cells = sources[h]
            identity = jnp.broadcast_to(jnp.arange(NB, dtype=jnp.int32)[None, :, None], (N_ROW, NB, 1))
            picks = jnp.concatenate([identity, cells[:, :, KP:]], axis=2)
            hit = (block[:, :, None, None] == jnp.arange(NB)[None, None, :, None]) & (
                k[None, :, None, None] == jnp.arange(KA)[None, None, None, :]
            )
            pick = jnp.sum(jnp.where(hit, picks[:, None], 0), axis=(2, 3))
            value = jnp.sum(
                jnp.where(pick[:, :, None] == jnp.arange(NB), cells[:, None, :, h] // N_COL, 0), axis=2
            )
            quotient = jnp.where(half[None, :] == h, value, quotient)
        result.append(u * N_ROW + quotient)
    return jnp.stack(result, axis=2).reshape(-1)


def shifted(value, axis, steps):
    count = lax.axis_size(axis)
    return lax.ppermute(value, axis, [(i, (i + steps) % count) for i in range(count)])


def shifted_plane(value, x_steps, y_steps):
    pairs = [
        (a * N_Y + b, (a + x_steps) % N_X * N_Y + (b + y_steps) % N_Y)
        for a in range(N_X)
        for b in range(N_Y)
    ]
    return lax.ppermute(value, COL, pairs)


def exchanged(value, axes):
    return lax.all_to_all(value, axes, split_axis=0, concat_axis=0, tiled=True)


META = KP + KA - 1
RELAYED = 5
LAST = 2


def product_tables(cells, x, y):
    groups = jnp.arange(GROUP, dtype=jnp.int32)
    columns = [x * N_Y + (y + groups) % N_Y]
    back = (y + groups) // N_Y
    e_x = jnp.stack([(x - back - k2) % N_X for k2 in range(PAIR)])
    columns.append((e_x * N_Y + y).reshape(-1))
    wanted = jnp.concatenate(columns)
    chosen = (wanted[:, None] == jnp.arange(N_COL, dtype=jnp.int32)[None, :]).astype(f32)
    found = jnp.dot(chosen, cells, precision=lax.Precision.HIGHEST)
    found = (found + 0.5).astype(jnp.int32).reshape(-1, NB, META)
    entry_row = (found[:GROUP, :, :KP] // N_COL).reshape(GROUP, NB * KP)
    order = jnp.arange(NB * KP, dtype=jnp.int32)
    slot = jnp.sum(
        (entry_row[:, None, :] == entry_row[:, :, None]) & (order[None, None, :] < order[None, :, None]),
        axis=2,
        dtype=jnp.int32,
    )
    picks = [jnp.arange(NB, dtype=jnp.int32)]
    for k in range(1, KA):
        picks.append(found[GROUP + k, :, KP + k - 1])
    picks = jnp.stack(picks).reshape(PAIR, GROUP, NB)
    offset = jnp.where(groups == 0, 0, (back[None, :] + jnp.arange(PAIR)[:, None]) * NB)
    picks = (picks + offset[:, :, None]).transpose(1, 0, 2).reshape(GROUP, PAIR * NB)
    return jnp.concatenate([entry_row, slot, e_x.T % 2, e_x.T // 2, picks], axis=1).reshape(-1)


def on_device(a_blocks, a_live, p_blocks, p_cols, ghost_list, policy, rates, rhs, guess):
    x = lax.axis_index("x")
    y = lax.axis_index("y")
    row = lax.axis_index(ROW)
    col = x * N_Y + y
    own_p = p_blocks.reshape(NB, BS * KP, CB)
    p_one = shifted(own_p, "x", 1)
    meta = jnp.concatenate([p_cols, ghost_list], axis=1).astype(f32).reshape(-1)
    cells = to_all(meta, COL, N_COL)
    spare = -(-N_COL * NB * META // NCOL)
    spare = -(-spare // 8) * 8
    padded = jnp.pad(cells.reshape(-1), (0, spare * NCOL - cells.size)).reshape(spare, NCOL)
    packed = to_all(jnp.concatenate([guess, padded]), ROW, N_ROW)
    around = packed[:, :CB].reshape(N_ROW * CB, NCOL)
    metas = packed[:, CB:].reshape(N_ROW, spare * NCOL)[:, : cells.size]
    metas = (metas + 0.5).astype(jnp.int32).reshape(N_ROW, N_COL, NB, META)

    p_back = shifted(own_p[RELAYED:], "x", -1)
    p_rear = shifted(p_back, "x", -1)
    p_far = shifted(p_one[:RELAYED], "x", 1)
    parts = None
    rate_rows = rates.reshape(-1, 1, BS)
    lefts = {}
    for group in (1, 3, 2, 0):
        left, parts = left_products(group, a_live, policy, a_blocks, rate_rows, own_p, parts)
        lefts[group] = shifted(left, "y", -group) if group else left
    table = product_tables(cells, x, y)
    where = places(metas, row, col).reshape(N_ROW, N_X, N_Y, 2)
    where = where // (N_Y * N_ROW) * N_ROW + where % N_ROW
    own_cell = x * N_ROW + row
    made = None
    stacked = None
    sums = []
    for batch in ((0,), (1, 3), (LAST,)):
        sent = None
        for lane, group in enumerate(batch):
            near, far = own_p, p_one
            if group:
                if stacked is None:
                    stacked = jnp.concatenate([own_p, p_one, p_far, p_rear])
                near = far = stacked
            sent = products(group, lane, len(batch), table, lefts[group], near, far, sent)
        got = exchanged(sent.reshape(N_ROW * N_X, len(batch), 2, CB, CB), PLANE)
        for lane, group in enumerate(batch):
            y_u = (y + group) % N_Y
            spots = lax.dynamic_index_in_dim(where, y_u, 2, False).reshape(-1)
            spots = jnp.concatenate([spots, jnp.stack([y_u, own_cell, x])])
            made, parts, floor = gather(group, lane, spots, got, around, made)
            if group == 0:
                floor_diag = floor
            if group != LAST:
                stack = jnp.stack(parts)
                sums.append(shifted(stack, "y", group) if group else stack)
    early = sums[0] + sums[1] + sums[2]
    applied = early[0]
    for d in range(1, N_X):
        applied = applied + shifted(early[d], "x", d)
    for d in range(N_X):
        applied = applied + shifted_plane(parts[d], d, LAST)
    current = guess + damping * (rhs - applied) / floor_diag

    coarse, *halves = made
    halves = [half.reshape(N_COL * CB, N_ROW * CB) for half in halves]
    part = apply(*halves, to_all(current, ROW, N_ROW).reshape(N_ROW * CB, NCOL))
    applied = jnp.sum(exchanged(part.reshape(N_COL, CB, NCOL), COL), axis=0)
    current = current + damping * (rhs - applied) / floor_diag
    return coarse.reshape(N_COL * CB, N_ROW, 1, CB), current


def solution(mesh):
    mesh = Mesh(mesh.devices.reshape(N_ROW // 2, 2, N_X, N_Y), ALL)

    return jax.shard_map(
        on_device,
        mesh=mesh,
        in_specs=(
            P(ALL, None, None, None),
            P(ALL, None),
            P(ALL, None, None, None),
            P(ALL, None),
            P(ALL, None),
            P(ALL),
            P(),
            P(ALL, None),
            P(ALL, None),
        ),
        out_specs=(P(ROW, None, COL, None), P(ALL, None)),
        check_vma=False,
    )
```

```python
import functools

import jax
import jax.numpy as jnp
from jax import lax
from jax.experimental import pallas as pl
from jax.experimental.pallas import tpu as pltpu
from jax.sharding import Mesh, PartitionSpec as P

BS = 256
CB = 128
KA = 8
KP = 2
N_ROW = 8
N_COL = 16
NB = 8
NCOL = 256
damping = 0.7
f32 = jnp.float32
bf16 = jnp.bfloat16
ROW = ("z", "core")
COL = ("x", "y")
ALL = ROW + COL
PLANE = ROW + ("x",)
N_X = N_Y = 4
GROUP = 4
LAST = 2
PAIR = 2


def split(value):
    high = value.astype(bf16)
    return high, (value - high.astype(f32)).astype(bf16)


def dot3(lhs, rhs):
    left = jnp.concatenate([lhs[0], lhs[0], lhs[1]], axis=1)
    right = jnp.concatenate([rhs[0], rhs[1], rhs[0]], axis=0)
    return jnp.dot(left, right, preferred_element_type=f32)


STEP = 2


def left_kernel(group, flips, live, policy, a_ref, *rest):
    rates = ()
    if group == 0:
        rates, rest = rest[:STEP], rest[STEP:]
    if flips:
        p_ref, out_ref, high_ref, low_ref = rest
    else:
        high_ref, low_ref, out_ref = rest
    step = pl.program_id(0)
    for r in range(STEP):
        s = step * STEP + r
        if flips:
            for m in range(KP):
                high, low = split(p_ref[r, pl.ds(m, BS, KP), :].T)
                high_ref[r, m * CB : (m + 1) * CB] = high
                low_ref[r, m * CB : (m + 1) * CB] = low
        for k2 in range(PAIR):
            block = a_ref[r, k2, 0] * live[s, group + GROUP * k2].astype(f32)
            if group == 0 and k2 == 0:
                across = lax.broadcasted_iota(jnp.int32, (BS, BS), 0)
                along = lax.broadcasted_iota(jnp.int32, (BS, BS), 1)
                block = block + jnp.where(across == along, rates[r][0], 0.0)
            out_ref[k2, r] = dot3((high_ref[r], low_ref[r]), split(block))


def left_products(group, live, policy, a_blocks, rates, own_p, parts):
    half = pl.BlockSpec((STEP, KP * CB, BS), lambda s, t, p: (s, 0, 0))
    halves = [jax.ShapeDtypeStruct((NB, KP * CB, BS), bf16)] * 2
    flips = parts is None
    rate = lambda r: pl.BlockSpec((1, 1, BS), lambda s, t, p: (p[s * STEP + r], 0, 0))
    results = pl.pallas_call(
        functools.partial(left_kernel, group, flips),
        grid_spec=pltpu.PrefetchScalarGridSpec(
            num_scalar_prefetch=2,
            grid=(NB // STEP,),
            in_specs=[pl.BlockSpec((STEP, PAIR, 1, BS, BS), lambda s, t, p: (s, 0, group, 0, 0))]
            + ([rate(r) for r in range(STEP)] if group == 0 else [])
            + ([pl.BlockSpec((STEP, KP * BS, CB), lambda s, t, p: (s, 0, 0))] if flips else [half, half]),
            out_specs=[pl.BlockSpec((PAIR, STEP, KP * CB, BS), lambda s, t, p: (0, s, 0, 0))]
            + ([half, half] if flips else []),
        ),
        out_shape=[jax.ShapeDtypeStruct((PAIR, NB, KP * CB, BS), f32)] + (halves if flips else []),
        cost_estimate=pl.CostEstimate(
            flops=NB * PAIR * 3 * 2 * BS**3,
            bytes_accessed=4 * PAIR * NB * 3 * BS * BS,
            transcendentals=0,
        ),
    )(
        live,
        policy,
        a_blocks.reshape(NB, PAIR, GROUP, BS, BS),
        *([rates] * STEP if group == 0 else []),
        *([own_p] if flips else parts),
    )
    return results[0], (list(results[1:]) if flips else parts)


ROW_AT, SLOT_AT, PARITY_AT, HALF_AT, PICK_AT, TABLE = 0, 16, 32, 34, 36, 52


def product_kernel(base, lane, table, t_ref, *rest):
    sources, (out_ref, held, sems) = rest[: PAIR * STEP], rest[-3:]
    step = pl.program_id(0)

    def copy(step, r, m):
        entry = (step * STEP + r) * KP + m
        return pltpu.make_async_copy(
            held.at[lax.rem(step, 2), r, m],
            out_ref.at[table[base + ROW_AT + entry], :, :, lane, table[base + SLOT_AT + entry]],
            sems.at[lax.rem(step, 2), r, m],
        )

    def each(step, act):
        for r in range(STEP):
            for m in range(KP):
                act(copy(step, r, m))

    @pl.when(step >= 2)
    def _():
        each(step - 2, lambda c: c.wait())

    now = lax.rem(step, 2)
    for r in range(STEP):
        for k2 in range(PAIR):
            ref = sources[r * PAIR + k2]
            ghost = jnp.concatenate(
                [ref[0, pl.ds(0, BS, KP), :], ref[0, pl.ds(1, BS, KP), :]], axis=1
            )
            result = dot3(split(t_ref[k2, r]), split(ghost))
            half, parity = table[base + HALF_AT + k2], table[base + PARITY_AT + k2]
            for m in range(KP):
                held[now, r, m, half, parity] = result[m * CB : (m + 1) * CB, :CB]
                held[now, r, m, 1 - half, parity] = result[m * CB : (m + 1) * CB, CB:]
    each(step, lambda c: c.start())

    @pl.when(step == NB // STEP - 1)
    def _():
        each(NB // STEP - 2, lambda c: c.wait())
        each(NB // STEP - 1, lambda c: c.wait())


def products(group, lane, lanes, table, left, near, far, prior):
    before = [] if prior is None else [prior]
    base = group * TABLE
    source = lambda r, k2: pl.BlockSpec(
        (1, KP * BS, CB), lambda s, t: (t[base + PICK_AT + k2 * NB + s * STEP + r], 0, 0)
    )
    return pl.pallas_call(
        functools.partial(product_kernel, base, lane),
        grid_spec=pltpu.PrefetchScalarGridSpec(
            num_scalar_prefetch=1,
            grid=(NB // STEP,),
            in_specs=[pl.BlockSpec((PAIR, STEP, KP * CB, BS), lambda s, t: (0, s, 0, 0))]
            + [source(r, k2) for r in range(STEP) for k2 in range(PAIR)]
            + [pl.BlockSpec(memory_space=pl.ANY)] * len(before),
            out_specs=pl.BlockSpec(memory_space=pl.ANY),
            scratch_shapes=[
                pltpu.VMEM((2, STEP, KP, 2, 2, CB, CB), f32),
                pltpu.SemaphoreType.DMA((2, STEP, KP)),
            ],
        ),
        out_shape=jax.ShapeDtypeStruct((N_ROW, 2, 2, lanes, 2, CB, CB), f32),
        input_output_aliases={2 + PAIR * STEP: 0} if before else {},
        cost_estimate=pl.CostEstimate(
            flops=NB * PAIR * 3 * 2 * BS**3,
            bytes_accessed=4 * PAIR * NB * 3 * BS * BS,
            transcendentals=0,
        ),
    )(table, left, *[near, far] * STEP, *before)


STEPS = 4
COUNT = 2 * N_ROW * N_X
PER_STEP = COUNT // STEPS
CELLS = N_X * N_ROW


def gather_kernel(group, table, got_ref, x_ref, *rest):
    made = N_X if group == LAST else 1
    coarse_ref, high_ref, low_ref, *part_refs, floor_ref, total, x_high, x_low = rest[-(made + 7) :]
    step = pl.program_id(0)

    @pl.when(step == 0)
    def _():
        total[...] = jnp.zeros_like(total)
        high, low = split(x_ref[...])
        x_high[...] = high
        x_low[...] = low

    @pl.loop(0, PER_STEP, step=4)
    def _(first):
        for b in range(4):
            place = table[step * PER_STEP + first + b]
            total[place] += got_ref[first // 2 + b // 2, 0, b % 2]

    def finish(ds):
        rows = []
        for d in ds:
            u = lax.rem(table[COUNT + 2] + d, N_X)
            blocks = [total[u * N_ROW + q] for q in range(N_ROW)]
            for q in range(N_ROW):
                coarse_ref[u, 0, pl.ds(q, CB, N_ROW), :] = blocks[q]
            rows.append(jnp.concatenate(blocks, axis=1))
        high, low = split(jnp.concatenate(rows))
        result = dot3((high, low), (x_high[...], x_low[...]))
        for i, d in enumerate(ds):
            u = lax.rem(table[COUNT + 2] + d, N_X)
            mine = slice(i * CB, (i + 1) * CB)
            high_ref[u, 0] = high[mine]
            low_ref[u, 0] = low[mine]
            if len(ds) == 1:
                part_refs[0][d] = result
            else:
                part_refs[d][...] = result[mine]

    @pl.when(step == STEPS - 1)
    def _():
        if group == LAST:
            finish(range(N_X))
        else:
            pl.loop(0, N_X)(lambda d: finish([d]))
        if group == 0:
            across = lax.broadcasted_iota(jnp.int32, (CB, CB), 0)
            along = lax.broadcasted_iota(jnp.int32, (CB, CB), 1)
            own = jnp.where(across == along, total[table[COUNT + 1]], 0.0)
            diag = jnp.maximum(jnp.abs(jnp.sum(own, axis=1, keepdims=True)), 1.0)
            floor_ref[...] = jnp.broadcast_to(diag, (CB, NCOL))


def gather(group, lane, table, got, x, prior):
    whole = lambda shape: pl.BlockSpec(shape, lambda i, t: (0,) * len(shape))
    in_specs = [
        pl.BlockSpec((PER_STEP // 2, 1, 2, CB, CB), lambda i, t: (i, lane, 0, 0, 0)),
        whole((N_ROW * CB, NCOL)),
    ]
    args = [got, x]
    alias = {}
    if prior is not None:
        in_specs += [pl.BlockSpec(memory_space=pl.ANY)] * len(prior)
        args += prior
        alias = {3: 0, 4: 1, 5: 2}
    shapes = [(CB, NCOL)] * N_X if group == LAST else [(N_X, CB, NCOL)]
    shapes.append((CB, NCOL))
    rows = pl.BlockSpec((N_X, 1, CB, N_ROW * CB), lambda i, t: (0, t[COUNT], 0, 0))
    *made, floor = pl.pallas_call(
        functools.partial(gather_kernel, group),
        grid_spec=pltpu.PrefetchScalarGridSpec(
            num_scalar_prefetch=1,
            grid=(STEPS,),
            in_specs=in_specs,
            out_specs=[pl.BlockSpec((N_X, 1, CB * N_ROW, CB), lambda i, t: (0, t[COUNT], 0, 0)), rows, rows]
            + [whole(shape) for shape in shapes],
            scratch_shapes=[
                pltpu.VMEM((CELLS, CB, CB), f32),
                pltpu.VMEM((N_ROW * CB, NCOL), bf16),
                pltpu.VMEM((N_ROW * CB, NCOL), bf16),
            ],
        ),
        out_shape=[jax.ShapeDtypeStruct((N_X, N_Y, CB * N_ROW, CB), f32)]
        + [jax.ShapeDtypeStruct((N_X, N_Y, CB, N_ROW * CB), bf16)] * 2
        + [jax.ShapeDtypeStruct(shape, f32) for shape in shapes],
        input_output_aliases=alias,
        cost_estimate=pl.CostEstimate(
            flops=3 * 2 * N_X * CB * N_ROW * CB * NCOL,
            bytes_accessed=4 * (COUNT + CELLS + 2 * CELLS) * CB * CB,
            transcendentals=0,
        ),
    )(table, *args)
    return made[:3], made[3:], floor


TALL = 4 * CB


def apply_kernel(table, high_ref, low_ref, same_ref, other_ref, *rest):
    out_ref, x_high, x_low = rest[-3:]

    @pl.when(pl.program_id(0) == 0)
    def _():
        core = table[1]
        for place, ref in ((core, same_ref), (1 - core, other_ref)):
            high, low = split(ref[...])
            x_high[place] = high
            x_low[place] = low

    right = (x_high[...].reshape(2 * CB, NCOL), x_low[...].reshape(2 * CB, NCOL))
    result = dot3((high_ref[...], low_ref[...]), right)
    if len(rest) > 3:
        result = result + rest[0][...]
    out_ref[...] = result


def apply(table, high, low, same, other, prior):
    wide = lambda shape: pl.BlockSpec(shape, lambda u, t: (u, 0))
    fixed = pl.BlockSpec((CB, NCOL), lambda u, t: (0, 0))
    columns = pl.BlockSpec((TALL, 2 * CB), lambda u, t: (u, t[0]))
    before = [] if prior is None else [prior]
    return pl.pallas_call(
        apply_kernel,
        grid_spec=pltpu.PrefetchScalarGridSpec(
            num_scalar_prefetch=1,
            grid=(N_COL * CB // TALL,),
            in_specs=[columns, columns, fixed, fixed] + [wide((TALL, NCOL))] * len(before),
            out_specs=wide((TALL, NCOL)),
            scratch_shapes=[pltpu.VMEM((2, CB, NCOL), bf16)] * 2,
        ),
        out_shape=jax.ShapeDtypeStruct((N_COL * CB, NCOL), f32),
        input_output_aliases={5: 0} if before else {},
        cost_estimate=pl.CostEstimate(
            flops=3 * 2 * N_COL * CB * 2 * CB * NCOL,
            bytes_accessed=4 * N_COL * CB * 4 * CB,
            transcendentals=0,
        ),
    )(table, high, low, same, other, *before)


def to_all(value, axes, count):
    copies = jnp.broadcast_to(value[None], (count,) + value.shape)
    return lax.all_to_all(copies, axes, split_axis=0, concat_axis=0, tiled=True)


def places(metas, row, col):
    delta = jnp.arange(N_COL, dtype=jnp.int32)
    p_cols = metas[:, :, :, :KP]
    entries = p_cols.reshape(N_ROW, N_COL, NB * KP)
    match = (entries // N_COL == row).astype(jnp.int32)
    earlier = jnp.cumsum(match, axis=2) - match
    order = jnp.arange(NB * KP, dtype=jnp.int32)
    sources = [
        lax.dynamic_index_in_dim(metas, (col + h * KA) % N_COL, 1, False) for h in range(2)
    ]
    result = []
    for t in range(2):
        chosen = match * (earlier == t)
        entry = jnp.sum(chosen * order, axis=2)
        u = jnp.sum(chosen * (entries % N_COL), axis=2)
        block = entry // KP
        far = (delta - col) % N_COL
        k, half = far % KA, far // KA
        quotient = jnp.zeros_like(u)
        for h in range(2):
            cells = sources[h]
            identity = jnp.broadcast_to(jnp.arange(NB, dtype=jnp.int32)[None, :, None], (N_ROW, NB, 1))
            picks = jnp.concatenate([identity, cells[:, :, KP:]], axis=2)
            hit = (block[:, :, None, None] == jnp.arange(NB)[None, None, :, None]) & (
                k[None, :, None, None] == jnp.arange(KA)[None, None, None, :]
            )
            pick = jnp.sum(jnp.where(hit, picks[:, None], 0), axis=(2, 3))
            value = jnp.sum(
                jnp.where(pick[:, :, None] == jnp.arange(NB), cells[:, None, :, h] // N_COL, 0), axis=2
            )
            quotient = jnp.where(half[None, :] == h, value, quotient)
        result.append(u * N_ROW + quotient)
    return jnp.stack(result, axis=2).reshape(-1)


def shifted(value, axis, steps):
    count = lax.axis_size(axis)
    return lax.ppermute(value, axis, [(i, (i + steps) % count) for i in range(count)])


def shifted_plane(value, x_steps, y_steps):
    pairs = [
        (a * N_Y + b, (a + x_steps) % N_X * N_Y + (b + y_steps) % N_Y)
        for a in range(N_X)
        for b in range(N_Y)
    ]
    return lax.ppermute(value, COL, pairs)


def shifted_row(value, z_steps, core_steps):
    pairs = [
        (a * 2 + b, (a + z_steps) % N_Z * 2 + (b + core_steps) % 2) for a in range(N_Z) for b in range(2)
    ]
    return lax.ppermute(value, ROW, pairs)


def exchanged(value, axes):
    return lax.all_to_all(value, axes, split_axis=0, concat_axis=0, tiled=True)


META = KP + KA - 1
RELAYED = 4
N_Z = 4
Z_ORDER = (0, 1, 3, 2)


def product_tables(cells, x, y):
    groups = jnp.arange(GROUP, dtype=jnp.int32)
    columns = [x * N_Y + (y + groups) % N_Y]
    back = (y + groups) // N_Y
    e_x = jnp.stack([(x - back - k2) % N_X for k2 in range(PAIR)])
    columns.append((e_x * N_Y + y).reshape(-1))
    wanted = jnp.concatenate(columns)
    chosen = (wanted[:, None] == jnp.arange(N_COL, dtype=jnp.int32)[None, :]).astype(f32)
    found = jnp.dot(chosen, cells, precision=lax.Precision.HIGHEST)
    found = (found + 0.5).astype(jnp.int32).reshape(-1, NB, META)
    entry_row = (found[:GROUP, :, :KP] // N_COL).reshape(GROUP, NB * KP)
    order = jnp.arange(NB * KP, dtype=jnp.int32)
    slot = jnp.sum(
        (entry_row[:, None, :] == entry_row[:, :, None]) & (order[None, None, :] < order[None, :, None]),
        axis=2,
        dtype=jnp.int32,
    )
    picks = [jnp.arange(NB, dtype=jnp.int32)]
    for k in range(1, KA):
        picks.append(found[GROUP + k, :, KP + k - 1])
    picks = jnp.stack(picks).reshape(PAIR, GROUP, NB)
    offset = jnp.where(groups == 0, 0, (back[None, :] + jnp.arange(PAIR)[:, None]) * NB)
    picks = (picks + offset[:, :, None]).transpose(1, 0, 2).reshape(GROUP, PAIR * NB)
    return jnp.concatenate([entry_row, slot, e_x.T % 2, e_x.T // 2, picks], axis=1).reshape(-1)


def on_device(a_blocks, a_live, p_blocks, p_cols, ghost_list, policy, rates, rhs, guess):
    x = lax.axis_index("x")
    y = lax.axis_index("y")
    row = lax.axis_index(ROW)
    col = x * N_Y + y
    own_p = p_blocks.reshape(NB, BS * KP, CB)
    p_one = shifted(own_p, "x", 1)
    meta = jnp.concatenate([p_cols, ghost_list], axis=1).astype(f32).reshape(-1)
    cells = to_all(meta, COL, N_COL)
    spare = -(-N_COL * NB * META // NCOL)
    spare = -(-spare // 8) * 8
    padded = jnp.pad(cells.reshape(-1), (0, spare * NCOL - cells.size)).reshape(spare, NCOL)
    packed = to_all(jnp.concatenate([guess, padded]), ROW, N_ROW)
    around = packed[:, :CB].reshape(N_ROW * CB, NCOL)
    metas = packed[:, CB:].reshape(N_ROW, spare * NCOL)[:, : cells.size]
    metas = (metas + 0.5).astype(jnp.int32).reshape(N_ROW, N_COL, NB, META)

    p_back = shifted(own_p[RELAYED:], "x", -1)
    p_rear = shifted(p_back, "x", -1)
    p_far = shifted(p_one[:RELAYED], "x", 1)
    parts = None
    rate_rows = rates.reshape(-1, 1, BS)
    lefts = {}
    for group in (1, 3, 2, 0):
        left, parts = left_products(group, a_live, policy, a_blocks, rate_rows, own_p, parts)
        lefts[group] = shifted(left, "y", -group) if group else left
    table = product_tables(cells, x, y)
    where = places(metas, row, col).reshape(N_ROW, N_X, N_Y, 2)
    where = where // (N_Y * N_ROW) * N_ROW + where % N_ROW
    own_cell = x * N_ROW + row
    made = None
    stacked = None
    sums = []
    for batch in ((0,), (1, 3), (LAST,)):
        sent = None
        for lane, group in enumerate(batch):
            near, far = own_p, p_one
            if group:
                if stacked is None:
                    stacked = jnp.concatenate([own_p, p_one, p_far, p_rear])
                near = far = stacked
            sent = products(group, lane, len(batch), table, lefts[group], near, far, sent)
        got = exchanged(sent.reshape(N_ROW * N_X, len(batch), 2, CB, CB), PLANE)
        for lane, group in enumerate(batch):
            y_u = (y + group) % N_Y
            spots = lax.dynamic_index_in_dim(where, y_u, 2, False).reshape(-1)
            spots = jnp.concatenate([spots, jnp.stack([y_u, own_cell, x])])
            made, parts, floor = gather(group, lane, spots, got, around, made)
            if group == 0:
                floor_diag = floor
            if group != LAST:
                sums.append(shifted(parts[0], "y", group) if group else parts[0])
    early = sums[0] + sums[1] + sums[2]
    applied = early[0]
    for d in range(1, N_X):
        applied = applied + shifted(early[d], "x", d)
    for d in range(N_X):
        applied = applied + shifted_plane(parts[d], d, LAST)
    current = guess + damping * (rhs - applied) / floor_diag

    coarse, *halves = made
    halves = [half.reshape(N_COL * CB, N_ROW * CB) for half in halves]
    z, core = lax.axis_index("z"), lax.axis_index("core")
    blocks = {}
    for dz in Z_ORDER:
        for dc in range(2):
            blocks[dz, dc] = shifted_row(current, dz, dc) if dz or dc else current
    part = None
    for dz in Z_ORDER:
        numbers = jnp.stack([(z - dz) % N_Z, core])
        part = apply(numbers, *halves, blocks[dz, 0], blocks[dz, 1], part)
    applied = jnp.sum(exchanged(part.reshape(N_COL, CB, NCOL), COL), axis=0)
    current = current + damping * (rhs - applied) / floor_diag
    return coarse.reshape(N_COL * CB, N_ROW, 1, CB), current


def solution(mesh):
    mesh = Mesh(mesh.devices.reshape(N_ROW // 2, 2, N_X, N_Y), ALL)

    return jax.shard_map(
        on_device,
        mesh=mesh,
        in_specs=(
            P(ALL, None, None, None),
            P(ALL, None),
            P(ALL, None, None, None),
            P(ALL, None),
            P(ALL, None),
            P(ALL),
            P(),
            P(ALL, None),
            P(ALL, None),
        ),
        out_specs=(P(ROW, None, COL, None), P(ALL, None)),
        check_vma=False,
    )
```

```python
import functools

import jax
import jax.numpy as jnp
from jax import lax
from jax.experimental import pallas as pl
from jax.experimental.pallas import tpu as pltpu
from jax.sharding import Mesh, PartitionSpec as P

BS = 256
CB = 128
KA = 8
KP = 2
N_ROW = 8
N_COL = 16
NB = 8
NCOL = 256
damping = 0.7
f32 = jnp.float32
bf16 = jnp.bfloat16
ROW = ("z", "core")
COL = ("x", "y")
ALL = ROW + COL
PLANE = ROW + ("x",)
N_X = N_Y = 4
GROUP = 4
LAST = 2
PAIR = 2


def split(value):
    high = value.astype(bf16)
    return high, (value - high.astype(f32)).astype(bf16)


def dot3(lhs, rhs):
    left = jnp.concatenate([lhs[0], lhs[0], lhs[1]], axis=1)
    right = jnp.concatenate([rhs[0], rhs[1], rhs[0]], axis=0)
    return jnp.dot(left, right, preferred_element_type=f32)


STEP = 2


def left_kernel(group, flips, live, policy, a_ref, *rest):
    rates = ()
    if group == 0:
        rates, rest = rest[:STEP], rest[STEP:]
    if flips:
        p_ref, out_ref, high_ref, low_ref = rest
    else:
        high_ref, low_ref, out_ref = rest
    step = pl.program_id(0)
    for r in range(STEP):
        s = step * STEP + r
        if flips:
            for m in range(KP):
                high, low = split(p_ref[r, pl.ds(m, BS, KP), :].T)
                high_ref[r, m * CB : (m + 1) * CB] = high
                low_ref[r, m * CB : (m + 1) * CB] = low
        for k2 in range(PAIR):
            block = a_ref[r, k2, 0] * live[s, group + GROUP * k2].astype(f32)
            if group == 0 and k2 == 0:
                across = lax.broadcasted_iota(jnp.int32, (BS, BS), 0)
                along = lax.broadcasted_iota(jnp.int32, (BS, BS), 1)
                block = block + jnp.where(across == along, rates[r][0], 0.0)
            out_ref[k2, r] = dot3((high_ref[r], low_ref[r]), split(block))


def left_products(group, live, policy, a_blocks, rates, own_p, parts):
    half = pl.BlockSpec((STEP, KP * CB, BS), lambda s, t, p: (s, 0, 0))
    halves = [jax.ShapeDtypeStruct((NB, KP * CB, BS), bf16)] * 2
    flips = parts is None
    rate = lambda r: pl.BlockSpec((1, 1, BS), lambda s, t, p: (p[s * STEP + r], 0, 0))
    results = pl.pallas_call(
        functools.partial(left_kernel, group, flips),
        grid_spec=pltpu.PrefetchScalarGridSpec(
            num_scalar_prefetch=2,
            grid=(NB // STEP,),
            in_specs=[pl.BlockSpec((STEP, PAIR, 1, BS, BS), lambda s, t, p: (s, 0, group, 0, 0))]
            + ([rate(r) for r in range(STEP)] if group == 0 else [])
            + ([pl.BlockSpec((STEP, KP * BS, CB), lambda s, t, p: (s, 0, 0))] if flips else [half, half]),
            out_specs=[pl.BlockSpec((PAIR, STEP, KP * CB, BS), lambda s, t, p: (0, s, 0, 0))]
            + ([half, half] if flips else []),
        ),
        out_shape=[jax.ShapeDtypeStruct((PAIR, NB, KP * CB, BS), f32)] + (halves if flips else []),
        cost_estimate=pl.CostEstimate(
            flops=NB * PAIR * 3 * 2 * BS**3,
            bytes_accessed=4 * PAIR * NB * 3 * BS * BS,
            transcendentals=0,
        ),
    )(
        live,
        policy,
        a_blocks.reshape(NB, PAIR, GROUP, BS, BS),
        *([rates] * STEP if group == 0 else []),
        *([own_p] if flips else parts),
    )
    return results[0], (list(results[1:]) if flips else parts)


ROW_AT, SLOT_AT, PARITY_AT, HALF_AT, PICK_AT, TABLE = 0, 16, 32, 34, 36, 52


def product_kernel(base, lane, table, t_ref, *rest):
    sources, (out_ref, held, sems) = rest[: PAIR * STEP], rest[-3:]
    step = pl.program_id(0)

    def copy(step, r, m):
        entry = (step * STEP + r) * KP + m
        return pltpu.make_async_copy(
            held.at[lax.rem(step, 2), r, m],
            out_ref.at[table[base + ROW_AT + entry], :, :, lane, table[base + SLOT_AT + entry]],
            sems.at[lax.rem(step, 2), r, m],
        )

    def each(step, act):
        for r in range(STEP):
            for m in range(KP):
                act(copy(step, r, m))

    @pl.when(step >= 2)
    def _():
        each(step - 2, lambda c: c.wait())

    now = lax.rem(step, 2)
    for r in range(STEP):
        for k2 in range(PAIR):
            ref = sources[r * PAIR + k2]
            ghost = jnp.concatenate(
                [ref[0, pl.ds(0, BS, KP), :], ref[0, pl.ds(1, BS, KP), :]], axis=1
            )
            result = dot3(split(t_ref[k2, r]), split(ghost))
            half, parity = table[base + HALF_AT + k2], table[base + PARITY_AT + k2]
            for m in range(KP):
                held[now, r, m, half, parity] = result[m * CB : (m + 1) * CB, :CB]
                held[now, r, m, 1 - half, parity] = result[m * CB : (m + 1) * CB, CB:]
    each(step, lambda c: c.start())

    @pl.when(step == NB // STEP - 1)
    def _():
        each(NB // STEP - 2, lambda c: c.wait())
        each(NB // STEP - 1, lambda c: c.wait())


def products(group, lane, lanes, table, left, near, far, prior):
    before = [] if prior is None else [prior]
    base = group * TABLE
    source = lambda r, k2: pl.BlockSpec(
        (1, KP * BS, CB), lambda s, t: (t[base + PICK_AT + k2 * NB + s * STEP + r], 0, 0)
    )
    return pl.pallas_call(
        functools.partial(product_kernel, base, lane),
        grid_spec=pltpu.PrefetchScalarGridSpec(
            num_scalar_prefetch=1,
            grid=(NB // STEP,),
            in_specs=[pl.BlockSpec((PAIR, STEP, KP * CB, BS), lambda s, t: (0, s, 0, 0))]
            + [source(r, k2) for r in range(STEP) for k2 in range(PAIR)]
            + [pl.BlockSpec(memory_space=pl.ANY)] * len(before),
            out_specs=pl.BlockSpec(memory_space=pl.ANY),
            scratch_shapes=[
                pltpu.VMEM((2, STEP, KP, 2, 2, CB, CB), f32),
                pltpu.SemaphoreType.DMA((2, STEP, KP)),
            ],
        ),
        out_shape=jax.ShapeDtypeStruct((N_ROW, 2, 2, lanes, 2, CB, CB), f32),
        input_output_aliases={2 + PAIR * STEP: 0} if before else {},
        cost_estimate=pl.CostEstimate(
            flops=NB * PAIR * 3 * 2 * BS**3,
            bytes_accessed=4 * PAIR * NB * 3 * BS * BS,
            transcendentals=0,
        ),
    )(table, left, *[near, far] * STEP, *before)


STEPS = 4
COUNT = 2 * N_ROW * N_X
PER_STEP = COUNT // STEPS
CELLS = N_X * N_ROW


def gather_kernel(group, table, got_ref, x_ref, *rest):
    made = N_X if group == LAST else 1
    coarse_ref, high_ref, low_ref, *part_refs, floor_ref, total, x_high, x_low = rest[-(made + 7) :]
    step = pl.program_id(0)

    @pl.when(step == 0)
    def _():
        total[...] = jnp.zeros_like(total)
        high, low = split(x_ref[...])
        x_high[...] = high
        x_low[...] = low

    @pl.loop(0, PER_STEP, step=4)
    def _(first):
        for b in range(4):
            place = table[step * PER_STEP + first + b]
            total[place] += got_ref[first // 2 + b // 2, 0, b % 2]

    def finish(ds):
        rows = []
        for d in ds:
            u = lax.rem(table[COUNT + 2] + d, N_X)
            blocks = [total[u * N_ROW + q] for q in range(N_ROW)]
            for q in range(N_ROW):
                coarse_ref[u, 0, pl.ds(q, CB, N_ROW), :] = blocks[q]
            rows.append(jnp.concatenate(blocks, axis=1))
        high, low = split(jnp.concatenate(rows))
        result = dot3((high, low), (x_high[...], x_low[...]))
        for i, d in enumerate(ds):
            u = lax.rem(table[COUNT + 2] + d, N_X)
            mine = slice(i * CB, (i + 1) * CB)
            high_ref[u, 0] = high[mine]
            low_ref[u, 0] = low[mine]
            if len(ds) == 1:
                part_refs[0][d] = result
            else:
                part_refs[d][...] = result[mine]

    @pl.when(step == STEPS - 1)
    def _():
        if group == LAST:
            finish(range(N_X))
        else:
            pl.loop(0, N_X)(lambda d: finish([d]))
        if group == 0:
            across = lax.broadcasted_iota(jnp.int32, (CB, CB), 0)
            along = lax.broadcasted_iota(jnp.int32, (CB, CB), 1)
            own = jnp.where(across == along, total[table[COUNT + 1]], 0.0)
            diag = jnp.maximum(jnp.abs(jnp.sum(own, axis=1, keepdims=True)), 1.0)
            floor_ref[...] = jnp.broadcast_to(diag, (CB, NCOL))


def gather(group, lane, table, got, x, prior):
    whole = lambda shape: pl.BlockSpec(shape, lambda i, t: (0,) * len(shape))
    in_specs = [
        pl.BlockSpec((PER_STEP // 2, 1, 2, CB, CB), lambda i, t: (i, lane, 0, 0, 0)),
        whole((N_ROW * CB, NCOL)),
    ]
    args = [got, x]
    alias = {}
    if prior is not None:
        in_specs += [pl.BlockSpec(memory_space=pl.ANY)] * len(prior)
        args += prior
        alias = {3: 0, 4: 1, 5: 2}
    shapes = [(CB, NCOL)] * N_X if group == LAST else [(N_X, CB, NCOL)]
    shapes.append((CB, NCOL))
    rows = pl.BlockSpec((N_X, 1, CB, N_ROW * CB), lambda i, t: (0, t[COUNT], 0, 0))
    *made, floor = pl.pallas_call(
        functools.partial(gather_kernel, group),
        grid_spec=pltpu.PrefetchScalarGridSpec(
            num_scalar_prefetch=1,
            grid=(STEPS,),
            in_specs=in_specs,
            out_specs=[pl.BlockSpec((N_X, 1, CB * N_ROW, CB), lambda i, t: (0, t[COUNT], 0, 0)), rows, rows]
            + [whole(shape) for shape in shapes],
            scratch_shapes=[
                pltpu.VMEM((CELLS, CB, CB), f32),
                pltpu.VMEM((N_ROW * CB, NCOL), bf16),
                pltpu.VMEM((N_ROW * CB, NCOL), bf16),
            ],
        ),
        out_shape=[jax.ShapeDtypeStruct((N_X, N_Y, CB * N_ROW, CB), f32)]
        + [jax.ShapeDtypeStruct((N_X, N_Y, CB, N_ROW * CB), bf16)] * 2
        + [jax.ShapeDtypeStruct(shape, f32) for shape in shapes],
        input_output_aliases=alias,
        cost_estimate=pl.CostEstimate(
            flops=3 * 2 * N_X * CB * N_ROW * CB * NCOL,
            bytes_accessed=4 * (COUNT + CELLS + 2 * CELLS) * CB * CB,
            transcendentals=0,
        ),
    )(table, *args)
    return made[:3], made[3:], floor


TALL = 4 * CB


def apply_kernel(table, high_ref, low_ref, *rest):
    blocks, (out_ref, x_high, x_low) = rest[:N_ROW], rest[N_ROW:]

    @pl.when(pl.program_id(0) == 0)
    def _():
        for i, ref in enumerate(blocks):
            high, low = split(ref[...])
            x_high[table[i]] = high
            x_low[table[i]] = low

    right = (x_high[...].reshape(N_ROW * CB, NCOL), x_low[...].reshape(N_ROW * CB, NCOL))
    out_ref[...] = dot3((high_ref[...], low_ref[...]), right)


def apply(table, high, low, blocks):
    rows = pl.BlockSpec((TALL, N_ROW * CB), lambda u, t: (u, 0))
    return pl.pallas_call(
        apply_kernel,
        grid_spec=pltpu.PrefetchScalarGridSpec(
            num_scalar_prefetch=1,
            grid=(N_COL * CB // TALL,),
            in_specs=[rows, rows] + [pl.BlockSpec((CB, NCOL), lambda u, t: (0, 0))] * N_ROW,
            out_specs=pl.BlockSpec((TALL, NCOL), lambda u, t: (u, 0)),
            scratch_shapes=[pltpu.VMEM((N_ROW, CB, NCOL), bf16)] * 2,
        ),
        out_shape=jax.ShapeDtypeStruct((N_COL * CB, NCOL), f32),
    )(table, high, low, *blocks)


def to_all(value, axes, count):
    copies = jnp.broadcast_to(value[None], (count,) + value.shape)
    return lax.all_to_all(copies, axes, split_axis=0, concat_axis=0, tiled=True)


def places(metas, row, col):
    delta = jnp.arange(N_COL, dtype=jnp.int32)
    p_cols = metas[:, :, :, :KP]
    entries = p_cols.reshape(N_ROW, N_COL, NB * KP)
    match = (entries // N_COL == row).astype(jnp.int32)
    earlier = jnp.cumsum(match, axis=2) - match
    order = jnp.arange(NB * KP, dtype=jnp.int32)
    sources = [
        lax.dynamic_index_in_dim(metas, (col + h * KA) % N_COL, 1, False) for h in range(2)
    ]
    result = []
    for t in range(2):
        chosen = match * (earlier == t)
        entry = jnp.sum(chosen * order, axis=2)
        u = jnp.sum(chosen * (entries % N_COL), axis=2)
        block = entry // KP
        far = (delta - col) % N_COL
        k, half = far % KA, far // KA
        quotient = jnp.zeros_like(u)
        for h in range(2):
            cells = sources[h]
            identity = jnp.broadcast_to(jnp.arange(NB, dtype=jnp.int32)[None, :, None], (N_ROW, NB, 1))
            picks = jnp.concatenate([identity, cells[:, :, KP:]], axis=2)
            hit = (block[:, :, None, None] == jnp.arange(NB)[None, None, :, None]) & (
                k[None, :, None, None] == jnp.arange(KA)[None, None, None, :]
            )
            pick = jnp.sum(jnp.where(hit, picks[:, None], 0), axis=(2, 3))
            value = jnp.sum(
                jnp.where(pick[:, :, None] == jnp.arange(NB), cells[:, None, :, h] // N_COL, 0), axis=2
            )
            quotient = jnp.where(half[None, :] == h, value, quotient)
        result.append(u * N_ROW + quotient)
    return jnp.stack(result, axis=2).reshape(-1)


def shifted(value, axis, steps):
    count = lax.axis_size(axis)
    return lax.ppermute(value, axis, [(i, (i + steps) % count) for i in range(count)])


def shifted_plane(value, x_steps, y_steps):
    pairs = [
        (a * N_Y + b, (a + x_steps) % N_X * N_Y + (b + y_steps) % N_Y)
        for a in range(N_X)
        for b in range(N_Y)
    ]
    return lax.ppermute(value, COL, pairs)


def shifted_row(value, z_steps, core_steps):
    pairs = [
        (a * 2 + b, (a + z_steps) % N_Z * 2 + (b + core_steps) % 2) for a in range(N_Z) for b in range(2)
    ]
    return lax.ppermute(value, ROW, pairs)


def exchanged(value, axes):
    return lax.all_to_all(value, axes, split_axis=0, concat_axis=0, tiled=True)


META = KP + KA - 1
RELAYED = 4
N_Z = 4
Z_ORDER = (0, 1, 3, 2)


def product_tables(cells, x, y):
    groups = jnp.arange(GROUP, dtype=jnp.int32)
    columns = [x * N_Y + (y + groups) % N_Y]
    back = (y + groups) // N_Y
    e_x = jnp.stack([(x - back - k2) % N_X for k2 in range(PAIR)])
    columns.append((e_x * N_Y + y).reshape(-1))
    wanted = jnp.concatenate(columns)
    chosen = (wanted[:, None] == jnp.arange(N_COL, dtype=jnp.int32)[None, :]).astype(f32)
    found = jnp.dot(chosen, cells, precision=lax.Precision.HIGHEST)
    found = (found + 0.5).astype(jnp.int32).reshape(-1, NB, META)
    entry_row = (found[:GROUP, :, :KP] // N_COL).reshape(GROUP, NB * KP)
    order = jnp.arange(NB * KP, dtype=jnp.int32)
    slot = jnp.sum(
        (entry_row[:, None, :] == entry_row[:, :, None]) & (order[None, None, :] < order[None, :, None]),
        axis=2,
        dtype=jnp.int32,
    )
    picks = [jnp.arange(NB, dtype=jnp.int32)]
    for k in range(1, KA):
        picks.append(found[GROUP + k, :, KP + k - 1])
    picks = jnp.stack(picks).reshape(PAIR, GROUP, NB)
    offset = jnp.where(groups == 0, 0, (back[None, :] + jnp.arange(PAIR)[:, None]) * NB)
    picks = (picks + offset[:, :, None]).transpose(1, 0, 2).reshape(GROUP, PAIR * NB)
    return jnp.concatenate([entry_row, slot, e_x.T % 2, e_x.T // 2, picks], axis=1).reshape(-1)


def on_device(a_blocks, a_live, p_blocks, p_cols, ghost_list, policy, rates, rhs, guess):
    x = lax.axis_index("x")
    y = lax.axis_index("y")
    row = lax.axis_index(ROW)
    col = x * N_Y + y
    own_p = p_blocks.reshape(NB, BS * KP, CB)
    p_one = shifted(own_p, "x", 1)
    meta = jnp.concatenate([p_cols, ghost_list], axis=1).astype(f32).reshape(-1)
    cells = to_all(meta, COL, N_COL)
    spare = -(-N_COL * NB * META // NCOL)
    spare = -(-spare // 8) * 8
    padded = jnp.pad(cells.reshape(-1), (0, spare * NCOL - cells.size)).reshape(spare, NCOL)
    packed = to_all(jnp.concatenate([guess, padded]), ROW, N_ROW)
    around = packed[:, :CB].reshape(N_ROW * CB, NCOL)
    metas = packed[:, CB:].reshape(N_ROW, spare * NCOL)[:, : cells.size]
    metas = (metas + 0.5).astype(jnp.int32).reshape(N_ROW, N_COL, NB, META)

    p_back = shifted(own_p[RELAYED:], "x", -1)
    p_rear = shifted(p_back, "x", -1)
    p_far = shifted(p_one[:RELAYED], "x", 1)
    parts = None
    rate_rows = rates.reshape(-1, 1, BS)
    lefts = {}
    for group in (1, 3, 2, 0):
        left, parts = left_products(group, a_live, policy, a_blocks, rate_rows, own_p, parts)
        lefts[group] = shifted(left, "y", -group) if group else left
    table = product_tables(cells, x, y)
    where = places(metas, row, col).reshape(N_ROW, N_X, N_Y, 2)
    where = where // (N_Y * N_ROW) * N_ROW + where % N_ROW
    own_cell = x * N_ROW + row
    made = None
    stacked = None
    sums = []
    for batch in ((0,), (1, 3), (LAST,)):
        sent = None
        for lane, group in enumerate(batch):
            near, far = own_p, p_one
            if group:
                if stacked is None:
                    stacked = jnp.concatenate([own_p, p_one, p_far, p_rear])
                near = far = stacked
            sent = products(group, lane, len(batch), table, lefts[group], near, far, sent)
        got = exchanged(sent.reshape(N_ROW * N_X, len(batch), 2, CB, CB), PLANE)
        for lane, group in enumerate(batch):
            y_u = (y + group) % N_Y
            spots = lax.dynamic_index_in_dim(where, y_u, 2, False).reshape(-1)
            spots = jnp.concatenate([spots, jnp.stack([y_u, own_cell, x])])
            made, parts, floor = gather(group, lane, spots, got, around, made)
            if group == 0:
                floor_diag = floor
            if group != LAST:
                sums.append(shifted(parts[0], "y", group) if group else parts[0])
    early = sums[0] + sums[1] + sums[2]
    applied = early[0]
    for d in range(1, N_X):
        applied = applied + shifted(early[d], "x", d)
    for d in range(N_X):
        applied = applied + shifted_plane(parts[d], d, LAST)
    current = guess + damping * (rhs - applied) / floor_diag

    coarse, *halves = made
    halves = [half.reshape(N_COL * CB, N_ROW * CB) for half in halves]
    z, core = lax.axis_index("z"), lax.axis_index("core")
    blocks, owners = [], []
    for dz in Z_ORDER:
        for dc in range(2):
            blocks.append(shifted_row(current, dz, dc) if dz or dc else current)
            owners.append((z - dz) % N_Z * 2 + (core + dc) % 2)
    part = apply(jnp.stack(owners), *halves, blocks)
    applied = jnp.sum(exchanged(part.reshape(N_COL, CB, NCOL), COL), axis=0)
    current = current + damping * (rhs - applied) / floor_diag
    return coarse.reshape(N_COL * CB, N_ROW, 1, CB), current


def solution(mesh):
    mesh = Mesh(mesh.devices.reshape(N_ROW // 2, 2, N_X, N_Y), ALL)

    return jax.shard_map(
        on_device,
        mesh=mesh,
        in_specs=(
            P(ALL, None, None, None),
            P(ALL, None),
            P(ALL, None, None, None),
            P(ALL, None),
            P(ALL, None),
            P(ALL),
            P(),
            P(ALL, None),
            P(ALL, None),
        ),
        out_specs=(P(ROW, None, COL, None), P(ALL, None)),
        check_vma=False,
    )
```
